32 devices in a mesh: pole: 2 (over x), row: 8 (over z, y), col: 2 (over core).
Axes of the slice: x: 2, y: 2, z: 4, core: 2. Of those that a mesh axis runs over, the one named last changes fastest.
Arguments:
- inverse_pairs: bfloat16 [4, 12288, 12288], P('pole', 'row', 'col'), parts along dimension 0, may hold values from -0.09375 to 0.09375
- factor_rows: bfloat16 [4, 2, 2048, 256], P('pole', None, 'row', 'col'), parts along dimension 0, may hold values from -1.1953125 to 1.1953125
- diag_blocks: bfloat16 [4, 2, 256, 256], P('pole', None, None, 'col'), parts along dimension 0, may hold values from -6 to 6
- row_lists: int32 [2, 16], replicated, may hold values from 0 to 95, as said below
- block_order: int32 [96], replicated, may hold values from 0 to 95, each once
Outputs:
- inv_cols: float32 [4, 2, 12288, 256], P('pole', None, 'row', 'col'), parts along dimension 0
- schur_blocks: float32 [4, 2, 256, 256], P('pole', None, None, 'col'), parts along dimension 0
The draws below stay inside these ranges and needn't reach their ends.
There are 2 independent parts, one for each index of `pole`. The reference program is written for one: setup_inputs(seed, part) draws one part's arguments, and reference() takes and returns one part's arrays. A program takes and returns all parts, laid end to end along the dimension named above; an argument that names none is the same for every part. Nothing has to cross between parts.
Inputs may be any that keep to these rules, and one draw needn't show every extreme that they name: `row_lists`: each of the 2 rows holds 16 different block numbers in increasing order, always including 0 and 95.
All inputs are finite; a program needn't handle non-finite values.
Results may differ from the reference program's by a relative error of at most 0.0003.
Values may be sent and summed in bfloat16 or wider, within the bound.
A program may use at most 128 MiB of HBM per device.

```python
import jax
import jax.numpy as jnp
from jax import lax

NSN = 2
W = 256
MA = 12288
BLK = 128
R = 16
NB = 96
LROWS = 2048


def draw_row_lists(key, part):
    lists = []
    for supernode in range(NSN):
        inner = jax.random.permutation(jax.random.fold_in(key, 101 + supernode), NB - 2).astype(jnp.int32) + 1
        chosen = jnp.concatenate([jnp.zeros((1,), jnp.int32), inner[:R - 2], jnp.full((1,), NB - 1, jnp.int32)])
        lists.append(jnp.sort(chosen))
    return jnp.stack(lists).astype(jnp.int32)


def block_levels(rng, dims, cuts, least, high):
    factor_of = 1.0
    for axis_at, shards_of in cuts:
        steps = jax.random.uniform(jax.random.fold_in(jax.random.fold_in(rng, 6), axis_at), (shards_of,), jnp.float32, least / len(cuts), high / len(cuts))
        factor_of = factor_of * jnp.repeat(jnp.exp(steps), dims[axis_at] // shards_of).reshape((-1,) + (1,) * (len(dims) - 1 - axis_at))
    return factor_of


def normal_values(key, shape, deviation, bound, shards=(), held_as=jnp.bfloat16):
    result = deviation * jax.random.normal(key, shape, jnp.float32)
    if shards:
        result = result * block_levels(key, shape, shards, -0.22, 0.18)
    return jnp.clip(result, -bound, bound).astype(held_as)


def setup_inputs(seed: int = 0, part: int = 0) -> dict:
    splits = jax.random.split(jax.random.key(seed), 6)
    part_keys = jax.random.split(jax.random.fold_in(splits[5], part), 6)
    return {
        "inverse_pairs": normal_values(part_keys[0], (2, MA, MA), (2 * LROWS) ** -0.5, 0.09375, ((1, 8), (2, 2))),
        "factor_rows": normal_values(part_keys[1], (NSN, 2, LROWS, W), 0.2, 1.1953125, ((2, 8), (3, 2))),
        "diag_blocks": normal_values(part_keys[2], (NSN, 2, W, W), 1.0, 6.0, ((3, 2),)),
        "row_lists": draw_row_lists(jax.random.fold_in(splits[5], 71), part),
        "block_order": jax.random.permutation(splits[4], NB).astype(jnp.int32),
    }


def reference(inverse_pairs, factor_rows, diag_blocks, row_lists, block_order):
    columns = inverse_pairs.reshape(2, MA, NB, BLK)
    storage = jnp.arange(NB, dtype=jnp.int32)
    cols_list = []
    schur_list = []
    for supernode in range(NSN):
        hits = block_order[None, :] == row_lists[supernode][:, None]
        position = jnp.sum(jnp.where(hits, storage[None, :], 0), axis=1).astype(jnp.int32)
        chosen = jnp.take(columns, position, axis=2).reshape(2, MA, LROWS)
        factor = factor_rows[supernode]
        real_part = jnp.dot(chosen[0], factor[0], preferred_element_type=jnp.float32) - jnp.dot(chosen[1], factor[1], preferred_element_type=jnp.float32)
        imag_part = jnp.dot(chosen[0], factor[1], preferred_element_type=jnp.float32) + jnp.dot(chosen[1], factor[0], preferred_element_type=jnp.float32)
        values = -jnp.stack([real_part, imag_part])
        listed = jnp.take(values.reshape(2, NB, BLK, W), position, axis=1).reshape(2, LROWS, W)
        factor_wide = factor.astype(jnp.float32)
        highest = lax.Precision.HIGHEST
        gram_real = jnp.dot(factor_wide[0].T, listed[0], precision=highest) - jnp.dot(factor_wide[1].T, listed[1], precision=highest)
        gram_imag = jnp.dot(factor_wide[0].T, listed[1], precision=highest) + jnp.dot(factor_wide[1].T, listed[0], precision=highest)
        schur = diag_blocks[supernode].astype(jnp.float32) - jnp.stack([gram_real, gram_imag])
        cols_list.append(values)
        schur_list.append(schur)
    return jnp.stack(cols_list), jnp.stack(schur_list)
```

```python
import functools

import jax
import jax.numpy as jnp
from jax import lax
from jax.experimental import pallas as pl
from jax.experimental.pallas import tpu as pltpu
from jax.sharding import PartitionSpec as P

NSN = 2
BLK = 128
MESH = pl.DeviceIdType.MESH
ANY = pl.BlockSpec(memory_space=pl.ANY)
VMEM = pl.BlockSpec(memory_space=pltpu.VMEM)
SMEM = pl.BlockSpec(memory_space=pltpu.SMEM)


def aligned(start, size):
    return pl.ds(pl.multiple_of(start, size), size)


def index_tables(lists_s, order_s, lists_v, order_v, pick, keep, local_pick, local_keep, first, row, blocks_col, blocks_row):
    order = order_v[...]
    storage = lax.broadcasted_iota(jnp.int32, order.shape, 1)
    for k in range(lists_s.shape[0]):
        for j in range(lists_s.shape[1]):
            at = jnp.sum(jnp.where(order == lists_s[k, j], storage, 0)) - first
            inside = (at >= 0) & (at < blocks_col)
            pick[k, j] = jnp.clip(at, 0, blocks_col - 1)
            keep[k, j] = jnp.where(inside, 1.0, 0.0)
        listed = lists_v[k:k + 1, :]
        entry = lax.broadcasted_iota(jnp.int32, listed.shape, 1) + 1
        for t in range(blocks_row):
            found = jnp.sum(jnp.where(listed == order_s[0, row * blocks_row + t], entry, 0))
            local_pick[k, t] = jnp.clip(found - 1, 0, lists_s.shape[1] - 1)
            local_keep[k, t] = jnp.where(found > 0, 1.0, 0.0)


def kernel(n, ny, lists_s, order_s, lists_v, order_v, x_ref, a_ref, diag_ref, out_ref, sum_ref,
           pick, keep, local_pick, local_keep, a_buf, g_ref, own, oth, recv, bbuf, mine, parts, diag,
           a_sem, loc_sem, diag_sem, z_send, z_recv, y_send, y_recv, s_send, s_recv,
           v_send, v_recv, o_sem, r_send, r_recv, b_send, b_recv):
    nz = n // ny
    span = g_ref.shape[3] * BLK // n
    rows = a_ref.shape[1]
    blocks_col = a_ref.shape[2] // BLK
    blocks_row = rows // BLK
    tile = rows if rows <= 1536 else BLK
    per = max(1, span // BLK)
    unit = min(span, BLK)
    row = lax.axis_index("row")
    col = lax.axis_index("col")
    z = row // ny
    y = row % ny
    oy = ny - 1 - y
    sibling = {"col": 1 - col}
    up = {"row": row + ny}
    down = {"row": row - ny}
    across = {"row": z * ny + oy}
    size = sum_ref.shape[0] // (NSN * n)

    def place(k, r):
        return aligned(k * n * size + r * size, size)

    def stream(b):
        return pltpu.make_async_copy(a_ref.at[:, :, aligned(b * BLK, BLK)], a_buf.at[b], a_sem.at[b])

    def start_stream(b, carry):
        stream(b).start()
        return carry

    def wait_stream(b, carry):
        stream(b).wait()
        return carry

    def slot(c, k, r):
        if span >= BLK:
            return g_ref.at[c, k, :, pl.ds(r * per, per)]
        return g_ref.at[c, k, :, r * span // BLK, aligned(r * span % BLK, span)]

    def local(k):
        return pltpu.make_async_copy(x_ref.at[k], slot(col, k, row), loc_sem.at[k])

    def own_diag(k):
        return pltpu.make_async_copy(diag_ref.at[place(k, row)], diag.at[k], diag_sem.at[k])

    for k in range(NSN):
        local(k).start()
    lax.fori_loop(0, blocks_col, start_stream, 0)

    barrier = pltpu.get_barrier_semaphore()
    pl.semaphore_signal(barrier, inc=1, device_id=sibling, device_id_type=MESH)
    for d in range(1, n):
        pl.semaphore_signal(barrier, inc=1, device_id={"row": (row + d) % n}, device_id_type=MESH)
    pl.semaphore_wait(barrier, n)

    def copy(src, c, k, r, send, got, target):
        return pltpu.make_async_remote_copy(
            src_ref=src, dst_ref=slot(c, k, r), send_sem=send, recv_sem=got,
            device_id=target, device_id_type=MESH)

    def line(src, k, zz, target):
        return copy(src, col, k, zz * ny + y, z_send.at[k, zz], z_recv.at[k, zz], target)

    def side(src, k, zz, yy):
        return copy(src, col, k, zz * ny + yy, y_send.at[k, zz], y_recv.at[k, zz], across)

    def sib(src, c, k, r):
        return copy(src, c, k, r, s_send.at[k, r], s_recv.at[k, r], sibling)

    def here(k, zz, yy):
        return slot(col, k, zz * ny + yy)

    def first_up(k):
        return copy(x_ref.at[k], col, k, row, z_send.at[k, nz], z_recv.at[k, z], up)

    def first_down(k):
        return copy(x_ref.at[k], col, k, row, z_send.at[k, nz + 1], z_recv.at[k, z], down)

    for k in range(NSN):
        side(x_ref.at[k], k, z, y).start()
        pl.when(z < nz - 1)(lambda k=k: first_up(k).start())
        pl.when(z > 0)(lambda k=k: first_down(k).start())
        sib(x_ref.at[k], col, k, row).start()
    for k in range(NSN):
        own_diag(k).start()
    index_tables(lists_s, order_s, lists_v, order_v, pick, keep, local_pick, local_keep,
                 col * blocks_col, row, blocks_col, blocks_row)
    own[...] = jnp.zeros_like(own)
    oth[...] = jnp.zeros_like(oth)
    mine[...] = jnp.zeros_like(mine)
    for k in range(NSN):
        local(k).wait()

    def from_line(k, zz, forward, target):
        line(here(k, zz, y), k, zz, target).wait_recv()

        @pl.when(forward)
        def _():
            line(here(k, zz, y), k, zz, target).start()

        side(here(k, zz, y), k, zz, y).start()
        sib(here(k, zz, y), col, k, zz * ny + y).start()

    def from_side(k, zz):
        side(here(k, zz, oy), k, zz, oy).wait_recv()
        sib(here(k, zz, oy), col, k, zz * ny + oy).start()

    outs = (own, oth)

    def multiply(k, r):
        sib(slot(1 - col, k, r), 1 - col, k, r).wait_recv()
        if unit < BLK:
            bbuf[...] = jnp.zeros_like(bbuf)
        for e in range(per):
            start = r * span + e * BLK
            scale = keep[k, start // BLK]
            base = e * 2 * BLK
            if unit < BLK:
                shift = start % BLK
                top = aligned(base + shift, unit)
                low = aligned(base + BLK + shift, unit)
            else:
                top = pl.ds(base, unit)
                low = pl.ds(base + BLK, unit)
            for rel in range(2):
                c = col if rel == 0 else 1 - col
                at = pl.ds(0, unit) if unit == BLK else aligned(start % BLK, unit)
                real = (g_ref[c, k, 0, start // BLK, at, :].astype(jnp.float32) * scale).astype(jnp.bfloat16)
                imag = (g_ref[c, k, 1, start // BLK, at, :].astype(jnp.float32) * scale).astype(jnp.bfloat16)
                left = rel * 2 * BLK
                bbuf[top, left:left + BLK] = -real
                bbuf[top, left + BLK:left + 2 * BLK] = -imag
                bbuf[low, left:left + BLK] = imag
                bbuf[low, left + BLK:left + 2 * BLK] = -real

        def by_tile(t, inner):
            at = aligned(t * tile, tile)
            pieces = []
            for e in range(per):
                block = pick[k, (r * span + e * BLK) // BLK]
                pieces += [a_buf[block, 0, at, :], a_buf[block, 1, at, :]]
            left = jnp.concatenate(pieces, axis=1)
            for rel in range(2):
                found = jnp.dot(left, bbuf[:, rel * 2 * BLK:(rel + 1) * 2 * BLK],
                                preferred_element_type=jnp.float32)
                outs[rel][k, 0, at, :] += found[:, :BLK]
                outs[rel][k, 1, at, :] += found[:, BLK:]
            return inner

        lax.fori_loop(0, rows // tile, by_tile, 0)

    def swap(k):
        return pltpu.make_async_remote_copy(
            src_ref=oth.at[k], dst_ref=recv.at[k], send_sem=v_send.at[k], recv_sem=v_recv.at[k],
            device_id=sibling, device_id_type=MESH)

    steps = 2 * nz
    last = NSN + 4 * (steps - 1)

    def entry(e, carry):
        pl.when(e == last)(lambda: swap(0).start())
        g = (e - NSN) // 4
        q = (e - NSN) % 4
        away = g // 2 + 1 - q // 2
        mine_first = e < NSN
        k = jnp.where(mine_first, e, g % 2)
        zz = z + jnp.where(mine_first, 0, jnp.where(q % 2 == 0, -away, away))
        yy = jnp.where(mine_first | (q // 2 == 0), y, oy)
        valid = mine_first | ((zz >= 0) & (zz < nz) & ((away > 0) | (q % 2 == 0)))
        pl.when(valid)(lambda: multiply(k, zz * ny + yy))
        return carry

    def done_by(m):
        lag = jnp.where(m < 4, 2, jnp.where(m < steps - 1, 1, 0))
        return jnp.where(m < 1, 0, NSN + 4 * jnp.maximum(m - lag + 1, 0))

    def step(m, carry):
        d = m // 2 + 1
        k = m % 2
        pl.when(z - d >= 0)(lambda: from_line(k, z - d, z < nz - 1, up))
        pl.when(z + d < nz)(lambda: from_line(k, z + d, z > 0, down))
        pl.when(z - d + 1 >= 0)(lambda: from_side(k, z - d + 1))
        pl.when((d > 1) & (z + d - 1 < nz))(lambda: from_side(k, z + d - 1))
        pl.when(m == 1)(lambda: lax.fori_loop(0, blocks_col, wait_stream, None))
        lax.fori_loop(done_by(m - 1), done_by(m), entry, 0)
        return carry

    lax.fori_loop(0, steps, step, 0)
    swap(1).start()

    def scatter(k, d):
        to = (row + d) % n
        return pltpu.make_async_remote_copy(
            src_ref=mine.at[place(k, to)], dst_ref=parts.at[k, d],
            send_sem=r_send.at[k, d], recv_sem=r_recv.at[k, d],
            device_id={"row": to}, device_id_type=MESH)

    def spread(k, d):
        return pltpu.make_async_remote_copy(
            src_ref=parts.at[k, 0], dst_ref=sum_ref.at[place(k, row)],
            send_sem=b_send.at[k, d], recv_sem=b_recv.at[k, d],
            device_id={"row": (row + d) % n}, device_id_type=MESH)

    group = 3 if blocks_row % 3 == 0 else 1
    width = 2 * BLK
    for k in range(NSN):
        swap(k).wait_recv()
        own[k] += recv[k]
        pltpu.make_async_copy(own.at[k], out_ref.at[k], o_sem.at[k]).start()

        def correct(s, carry, k=k):
            left, right = [], []
            for u in range(group):
                t = s * group + u
                j = local_pick[k, t]
                scale = local_keep[k, t]
                for p in range(2):
                    left.append(jnp.concatenate([g_ref[0, k, p, j], g_ref[1, k, p, j]], axis=1))
                real = own[k, 0, aligned(t * BLK, BLK), :] * scale
                imag = own[k, 1, aligned(t * BLK, BLK), :] * scale
                right.append(jnp.concatenate([real, imag], axis=1))
                right.append(jnp.concatenate([-imag, real], axis=1))
            factor = jnp.concatenate(left, axis=0)
            wide = jnp.concatenate(right, axis=0)
            total = None
            for _ in range(2):
                piece = wide.astype(jnp.bfloat16)
                wide = wide - piece.astype(jnp.float32)
                term = lax.dot_general(factor, piece, (((0,), (0,)), ((), ())),
                                       preferred_element_type=jnp.float32)
                total = term if total is None else total + term
            mine[2 * k * width:(2 * k + 1) * width, :] += total[:, :BLK]
            mine[(2 * k + 1) * width:(2 * k + 2) * width, :] += total[:, BLK:]
            return carry

        lax.fori_loop(0, blocks_row // group, correct, 0)
        for d in range(1, n):
            scatter(k, d).start()

    for k in range(NSN):
        own_diag(k).wait()
        total = mine[place(k, row), :]
        for d in range(1, n):
            scatter(k, d).wait_recv()
            total = total + parts[k, d]
        total = diag[k].astype(jnp.float32) - total
        parts[k, 0] = total
        sum_ref[place(k, row), :] = total
        for d in range(1, n):
            spread(k, d).start()

    for k in range(NSN):
        for r in range(n):
            sib(slot(col, k, r), col, k, r).wait_send()
        for zz in range(nz):
            side(here(k, zz, y), k, zz, y).wait_send()
            pl.when(((zz < z) & (z < nz - 1)) | ((zz > z) & (z > 0)))(
                lambda k=k, zz=zz: line(here(k, zz, y), k, zz, up).wait_send())
        pl.when(z < nz - 1)(lambda k=k: first_up(k).wait_send())
        pl.when(z > 0)(lambda k=k: first_down(k).wait_send())
        swap(k).wait_send()
        pltpu.make_async_copy(own.at[k], out_ref.at[k], o_sem.at[k]).wait()
        for d in range(1, n):
            scatter(k, d).wait_send()
            spread(k, d).wait()


def local(n, inverse_pairs, factor_rows, diag_blocks, row_lists, block_order):
    rows, cols = inverse_pairs.shape[1:]
    blocks_row, blocks_col = rows // BLK, cols // BLK
    listed = row_lists.shape[1]
    order = block_order.reshape(1, -1)

    ny = 2 if n % 2 == 0 else 1
    nz = n // ny
    span, half = factor_rows.shape[2:]
    size = NSN * 2 * 2 * half
    per = max(1, span // BLK)
    shards = factor_rows.reshape(NSN, 2, per, BLK, half) if span >= BLK else factor_rows
    dma = pltpu.SemaphoreType.DMA
    side = (NSN, 2, rows, half)
    values, schur = pl.pallas_call(
        functools.partial(kernel, n, ny),
        out_shape=(jax.ShapeDtypeStruct(side, jnp.float32), jax.ShapeDtypeStruct((size, half), jnp.float32)),
        in_specs=[SMEM, SMEM, VMEM, VMEM, ANY, ANY, ANY],
        out_specs=(ANY, VMEM),
        scratch_shapes=[
            pltpu.SMEM((NSN, listed), jnp.int32),
            pltpu.SMEM((NSN, listed), jnp.float32),
            pltpu.SMEM((NSN, blocks_row), jnp.int32),
            pltpu.SMEM((NSN, blocks_row), jnp.float32),
            pltpu.VMEM((blocks_col, 2, rows, BLK), jnp.bfloat16),
            pltpu.VMEM((2, NSN, 2, listed, BLK, half), jnp.bfloat16),
            pltpu.VMEM(side, jnp.float32),
            pltpu.VMEM(side, jnp.float32),
            pltpu.VMEM(side, jnp.float32),
            pltpu.VMEM((per * 2 * BLK, 4 * BLK), jnp.bfloat16),
            pltpu.VMEM((size, half), jnp.float32),
            pltpu.VMEM((NSN, n, size // (NSN * n), half), jnp.float32),
            pltpu.VMEM((NSN, size // (NSN * n), half), jnp.bfloat16),
            dma((blocks_col,)), dma((NSN,)), dma((NSN,)), dma((NSN, nz + 2)), dma((NSN, nz)),
            dma((NSN, nz)), dma((NSN, nz)), dma((NSN, n)), dma((NSN, n)),
            dma((NSN,)), dma((NSN,)), dma((NSN,)), dma((NSN, n)), dma((NSN, n)), dma((NSN, n)), dma((NSN, n)),
        ],
        compiler_params=pltpu.CompilerParams(
            collective_id=0, has_side_effects=True, vmem_limit_bytes=66000000),
        name="inversion_step",
    )(row_lists, order, row_lists, order, shards, inverse_pairs, diag_blocks.reshape(size, half))
    return (values, schur.reshape(diag_blocks.shape))


def solution(mesh):
    in_specs = (
        P("pole", "row", "col"),
        P("pole", None, "row", "col"),
        P("pole", None, None, "col"),
        P(),
        P(),
    )
    out_specs = (P("pole", None, "row", "col"), P("pole", None, None, "col"))
    return jax.shard_map(functools.partial(local, mesh.shape["row"]), mesh=mesh, in_specs=in_specs,
                         out_specs=out_specs, check_vma=False)
```

```python
import functools

import jax
import jax.numpy as jnp
from jax import lax
from jax.experimental import pallas as pl
from jax.experimental.pallas import tpu as pltpu
from jax.sharding import PartitionSpec as P

NSN = 2
BLK = 128
MESH = pl.DeviceIdType.MESH
ANY = pl.BlockSpec(memory_space=pl.ANY)
VMEM = pl.BlockSpec(memory_space=pltpu.VMEM)
SMEM = pl.BlockSpec(memory_space=pltpu.SMEM)


def aligned(start, size):
    return pl.ds(pl.multiple_of(start, size), size)


def index_tables(lists_s, order_s, lists_v, order_v, pick, keep, local_pick, local_keep, first, row, blocks_col, blocks_row):
    order = order_v[...]
    storage = lax.broadcasted_iota(jnp.int32, order.shape, 1)
    for k in range(lists_s.shape[0]):
        for j in range(lists_s.shape[1]):
            at = jnp.sum(jnp.where(order == lists_s[k, j], storage, 0)) - first
            inside = (at >= 0) & (at < blocks_col)
            pick[k, j] = jnp.clip(at, 0, blocks_col - 1)
            keep[k, j] = jnp.where(inside, 1.0, 0.0)
        listed = lists_v[k:k + 1, :]
        entry = lax.broadcasted_iota(jnp.int32, listed.shape, 1) + 1
        for t in range(blocks_row):
            found = jnp.sum(jnp.where(listed == order_s[0, row * blocks_row + t], entry, 0))
            local_pick[k, t] = jnp.clip(found - 1, 0, lists_s.shape[1] - 1)
            local_keep[k, t] = jnp.where(found > 0, 1.0, 0.0)


def coded(value):
    most = jnp.maximum(jnp.max(jnp.abs(value), axis=0, keepdims=True), 1e-33)
    return jnp.round(value * (32767.0 / most)).astype(jnp.int32).astype(jnp.int16), most * (1.0 / 32767.0)


def decoded(code, scale):
    return code.astype(jnp.int32).astype(jnp.float32) * scale


def kernel(n, ny, lists_s, order_s, lists_v, order_v, x_ref, a_ref, diag_ref, out_ref, sum_ref,
           pick, keep, local_pick, local_keep, a_buf, g_ref, own, oth, recv, bbuf, mine, codes, scales, got_codes, got_scales, all_codes, all_scales, diag,
           a_sem, loc_sem, diag_sem, z_send, z_recv, y_send, y_recv, s_send, s_recv,
           v_send, v_recv, o_sem, r_send, r_recv, rs_send, rs_recv, b_send, b_recv, bs_send, bs_recv):
    nz = n // ny
    span = g_ref.shape[3] * BLK // n
    rows = a_ref.shape[1]
    blocks_col = a_ref.shape[2] // BLK
    blocks_row = rows // BLK
    tile = rows if rows <= 1536 else BLK
    per = max(1, span // BLK)
    unit = min(span, BLK)
    row = lax.axis_index("row")
    col = lax.axis_index("col")
    z = row // ny
    y = row % ny
    oy = ny - 1 - y
    sibling = {"col": 1 - col}
    up = {"row": row + ny}
    down = {"row": row - ny}
    across = {"row": z * ny + oy}
    size = sum_ref.shape[0] // (NSN * n)

    def place(k, r):
        return aligned(k * n * size + r * size, size)

    def stream(b):
        return pltpu.make_async_copy(a_ref.at[:, :, aligned(b * BLK, BLK)], a_buf.at[b], a_sem.at[b])

    def start_stream(b, carry):
        stream(b).start()
        return carry

    def wait_stream(b, carry):
        stream(b).wait()
        return carry

    def slot(c, k, r):
        if span >= BLK:
            return g_ref.at[c, k, :, pl.ds(r * per, per)]
        return g_ref.at[c, k, :, r * span // BLK, aligned(r * span % BLK, span)]

    def local(k):
        return pltpu.make_async_copy(x_ref.at[k], slot(col, k, row), loc_sem.at[k])

    def own_diag(k):
        return pltpu.make_async_copy(diag_ref.at[place(k, row)], diag.at[k], diag_sem.at[k])

    for k in range(NSN):
        local(k).start()
    lax.fori_loop(0, blocks_col, start_stream, 0)

    barrier = pltpu.get_barrier_semaphore()
    pl.semaphore_signal(barrier, inc=1, device_id=sibling, device_id_type=MESH)
    for d in range(1, n):
        pl.semaphore_signal(barrier, inc=1, device_id={"row": (row + d) % n}, device_id_type=MESH)
    pl.semaphore_wait(barrier, n)

    def copy(src, c, k, r, send, got, target):
        return pltpu.make_async_remote_copy(
            src_ref=src, dst_ref=slot(c, k, r), send_sem=send, recv_sem=got,
            device_id=target, device_id_type=MESH)

    def line(src, k, zz, target):
        return copy(src, col, k, zz * ny + y, z_send.at[k, zz], z_recv.at[k, zz], target)

    def side(src, k, zz, yy):
        return copy(src, col, k, zz * ny + yy, y_send.at[k, zz], y_recv.at[k, zz], across)

    def sib(src, c, k, r):
        return copy(src, c, k, r, s_send.at[k, r], s_recv.at[k, r], sibling)

    def here(k, zz, yy):
        return slot(col, k, zz * ny + yy)

    def first_up(k):
        return copy(x_ref.at[k], col, k, row, z_send.at[k, nz], z_recv.at[k, z], up)

    def first_down(k):
        return copy(x_ref.at[k], col, k, row, z_send.at[k, nz + 1], z_recv.at[k, z], down)

    for k in range(NSN):
        side(x_ref.at[k], k, z, y).start()
        pl.when(z < nz - 1)(lambda k=k: first_up(k).start())
        pl.when(z > 0)(lambda k=k: first_down(k).start())
        sib(x_ref.at[k], col, k, row).start()
    for k in range(NSN):
        own_diag(k).start()
    index_tables(lists_s, order_s, lists_v, order_v, pick, keep, local_pick, local_keep,
                 col * blocks_col, row, blocks_col, blocks_row)
    own[...] = jnp.zeros_like(own)
    oth[...] = jnp.zeros_like(oth)
    mine[...] = jnp.zeros_like(mine)
    for k in range(NSN):
        local(k).wait()

    def from_line(k, zz, forward, target):
        line(here(k, zz, y), k, zz, target).wait_recv()

        @pl.when(forward)
        def _():
            line(here(k, zz, y), k, zz, target).start()

        side(here(k, zz, y), k, zz, y).start()
        sib(here(k, zz, y), col, k, zz * ny + y).start()

    def from_side(k, zz):
        side(here(k, zz, oy), k, zz, oy).wait_recv()
        sib(here(k, zz, oy), col, k, zz * ny + oy).start()

    outs = (own, oth)

    def multiply(k, r):
        sib(slot(1 - col, k, r), 1 - col, k, r).wait_recv()
        if unit < BLK:
            bbuf[...] = jnp.zeros_like(bbuf)
        for e in range(per):
            start = r * span + e * BLK
            scale = keep[k, start // BLK]
            base = e * 2 * BLK
            if unit < BLK:
                shift = start % BLK
                top = aligned(base + shift, unit)
                low = aligned(base + BLK + shift, unit)
            else:
                top = pl.ds(base, unit)
                low = pl.ds(base + BLK, unit)
            for rel in range(2):
                c = col if rel == 0 else 1 - col
                at = pl.ds(0, unit) if unit == BLK else aligned(start % BLK, unit)
                real = (g_ref[c, k, 0, start // BLK, at, :].astype(jnp.float32) * scale).astype(jnp.bfloat16)
                imag = (g_ref[c, k, 1, start // BLK, at, :].astype(jnp.float32) * scale).astype(jnp.bfloat16)
                left = rel * 2 * BLK
                bbuf[top, left:left + BLK] = -real
                bbuf[top, left + BLK:left + 2 * BLK] = -imag
                bbuf[low, left:left + BLK] = imag
                bbuf[low, left + BLK:left + 2 * BLK] = -real

        def by_tile(t, inner):
            at = aligned(t * tile, tile)
            pieces = []
            for e in range(per):
                block = pick[k, (r * span + e * BLK) // BLK]
                pieces += [a_buf[block, 0, at, :], a_buf[block, 1, at, :]]
            left = jnp.concatenate(pieces, axis=1)
            for rel in range(2):
                found = jnp.dot(left, bbuf[:, rel * 2 * BLK:(rel + 1) * 2 * BLK],
                                preferred_element_type=jnp.float32)
                outs[rel][k, 0, at, :] += found[:, :BLK]
                outs[rel][k, 1, at, :] += found[:, BLK:]
            return inner

        lax.fori_loop(0, rows // tile, by_tile, 0)

    group = 3 if blocks_row % 3 == 0 else 1
    strips = blocks_row // group
    high = group * BLK

    def strip(k, s):
        return k, slice(None), aligned(s * high, high)

    def swap(k, s):
        return pltpu.make_async_remote_copy(
            src_ref=oth.at[strip(k, s)], dst_ref=recv.at[strip(k, s)], send_sem=v_send.at[k, s], recv_sem=v_recv.at[k, s],
            device_id=sibling, device_id_type=MESH)

    def start_swaps(k):
        def one(s, carry):
            swap(k, s).start()
            return carry
        lax.fori_loop(0, strips, one, 0)

    def put(k, s):
        return pltpu.make_async_copy(own.at[strip(k, s)], out_ref.at[strip(k, s)], o_sem.at[k, s])

    steps = 2 * nz
    last = NSN + 4 * (steps - 1)

    def entry(e, carry):
        pl.when(e == last)(lambda: start_swaps(0))
        g = (e - NSN) // 4
        q = (e - NSN) % 4
        away = g // 2 + 1 - q // 2
        mine_first = e < NSN
        k = jnp.where(mine_first, e, g % 2)
        zz = z + jnp.where(mine_first, 0, jnp.where(q % 2 == 0, -away, away))
        yy = jnp.where(mine_first | (q // 2 == 0), y, oy)
        valid = mine_first | ((zz >= 0) & (zz < nz) & ((away > 0) | (q % 2 == 0)))
        pl.when(valid)(lambda: multiply(k, zz * ny + yy))
        return carry

    def done_by(m):
        lag = jnp.where(m >= steps - 2, 0, jnp.where(m < 4, 2, 1))
        return jnp.where(m < 1, 0, NSN + 4 * jnp.maximum(m - lag + 1, 0))

    def step(m, carry):
        d = m // 2 + 1
        k = m % 2
        pl.when(z - d >= 0)(lambda: from_line(k, z - d, z < nz - 1, up))
        pl.when(z + d < nz)(lambda: from_line(k, z + d, z > 0, down))
        pl.when(z - d + 1 >= 0)(lambda: from_side(k, z - d + 1))
        pl.when((d > 1) & (z + d - 1 < nz))(lambda: from_side(k, z + d - 1))
        pl.when(m == 1)(lambda: lax.fori_loop(0, blocks_col, wait_stream, None))
        lax.fori_loop(done_by(m - 1), done_by(m), entry, 0)
        return carry

    lax.fori_loop(0, steps, step, 0)
    start_swaps(1)

    def scatter(k, d):
        to = (row + d) % n
        code = pltpu.make_async_remote_copy(
            src_ref=codes.at[k, to], dst_ref=got_codes.at[k, d],
            send_sem=r_send.at[k, d], recv_sem=r_recv.at[k, d],
            device_id={"row": to}, device_id_type=MESH)
        scale = pltpu.make_async_remote_copy(
            src_ref=scales.at[k, to], dst_ref=got_scales.at[k, d],
            send_sem=rs_send.at[k, d], recv_sem=rs_recv.at[k, d],
            device_id={"row": to}, device_id_type=MESH)
        return code, scale

    def spread(k, d, owner):
        to = (row + d) % n
        code = pltpu.make_async_remote_copy(
            src_ref=all_codes.at[k, owner], dst_ref=all_codes.at[k, owner],
            send_sem=b_send.at[k, d], recv_sem=b_recv.at[k, d],
            device_id={"row": to}, device_id_type=MESH)
        scale = pltpu.make_async_remote_copy(
            src_ref=all_scales.at[k, owner], dst_ref=all_scales.at[k, owner],
            send_sem=bs_send.at[k, d], recv_sem=bs_recv.at[k, d],
            device_id={"row": to}, device_id_type=MESH)
        return code, scale

    width = 2 * BLK
    for k in range(NSN):
        def correct(s, carry, k=k):
            swap(k, s).wait_recv()
            own[strip(k, s)] += recv[strip(k, s)]
            put(k, s).start()
            left, right = [], []
            for u in range(group):
                t = s * group + u
                j = local_pick[k, t]
                scale = local_keep[k, t]
                for p in range(2):
                    left.append(jnp.concatenate([g_ref[0, k, p, j], g_ref[1, k, p, j]], axis=1))
                real = own[k, 0, aligned(t * BLK, BLK), :] * scale
                imag = own[k, 1, aligned(t * BLK, BLK), :] * scale
                right.append(jnp.concatenate([real, imag], axis=1))
                right.append(jnp.concatenate([-imag, real], axis=1))
            factor = jnp.concatenate(left, axis=0)
            wide = jnp.concatenate(right, axis=0)
            total = None
            for _ in range(2):
                piece = wide.astype(jnp.bfloat16)
                wide = wide - piece.astype(jnp.float32)
                term = lax.dot_general(factor, piece, (((0,), (0,)), ((), ())),
                                       preferred_element_type=jnp.float32)
                total = term if total is None else total + term
            mine[2 * k * width:(2 * k + 1) * width, :] += total[:, :BLK]
            mine[(2 * k + 1) * width:(2 * k + 2) * width, :] += total[:, BLK:]
            return carry

        lax.fori_loop(0, strips, correct, 0)

        def encode(r, carry, k=k):
            codes[k, r], scales[k, r] = coded(mine[place(k, r), :])
            return carry

        lax.fori_loop(0, n, encode, 0)
        for d in range(1, n):
            for c in scatter(k, d):
                c.start()

    for k in range(NSN):
        own_diag(k).wait()
        total = mine[place(k, row), :]
        for d in range(1, n):
            for c in scatter(k, d):
                c.wait_recv()
            total = total + decoded(got_codes[k, d], got_scales[k, d])
        all_codes[k, row], all_scales[k, row] = coded(diag[k].astype(jnp.float32) - total)
        for d in range(1, n):
            for c in spread(k, d, row):
                c.start()

    for k in range(NSN):
        for r in range(n):
            sib(slot(col, k, r), col, k, r).wait_send()
        for zz in range(nz):
            side(here(k, zz, y), k, zz, y).wait_send()
            pl.when(((zz < z) & (z < nz - 1)) | ((zz > z) & (z > 0)))(
                lambda k=k, zz=zz: line(here(k, zz, y), k, zz, up).wait_send())
        pl.when(z < nz - 1)(lambda k=k: first_up(k).wait_send())
        pl.when(z > 0)(lambda k=k: first_down(k).wait_send())
        def drain(s, carry, k=k):
            swap(k, s).wait_send()
            put(k, s).wait()
            return carry

        lax.fori_loop(0, strips, drain, 0)
        for d in range(1, n):
            for c in scatter(k, d) + spread(k, d, row):
                c.wait_send()

    for k in range(NSN):
        for d in range(1, n):
            for c in spread(k, d, (row - d) % n):
                c.wait_recv()

        def decode(r, carry, k=k):
            sum_ref[place(k, r), :] = decoded(all_codes[k, r], all_scales[k, r])
            return carry

        lax.fori_loop(0, n, decode, 0)


def local(n, inverse_pairs, factor_rows, diag_blocks, row_lists, block_order):
    rows, cols = inverse_pairs.shape[1:]
    blocks_row, blocks_col = rows // BLK, cols // BLK
    listed = row_lists.shape[1]
    order = block_order.reshape(1, -1)

    ny = 2 if n % 2 == 0 else 1
    nz = n // ny
    span, half = factor_rows.shape[2:]
    size = NSN * 2 * 2 * half
    piece = size // (NSN * n)
    per = max(1, span // BLK)
    shards = factor_rows.reshape(NSN, 2, per, BLK, half) if span >= BLK else factor_rows
    dma = pltpu.SemaphoreType.DMA
    side = (NSN, 2, rows, half)
    values, schur = pl.pallas_call(
        functools.partial(kernel, n, ny),
        out_shape=(jax.ShapeDtypeStruct(side, jnp.float32), jax.ShapeDtypeStruct((size, half), jnp.float32)),
        in_specs=[SMEM, SMEM, VMEM, VMEM, ANY, ANY, ANY],
        out_specs=(ANY, VMEM),
        scratch_shapes=[
            pltpu.SMEM((NSN, listed), jnp.int32),
            pltpu.SMEM((NSN, listed), jnp.float32),
            pltpu.SMEM((NSN, blocks_row), jnp.int32),
            pltpu.SMEM((NSN, blocks_row), jnp.float32),
            pltpu.VMEM((blocks_col, 2, rows, BLK), jnp.bfloat16),
            pltpu.VMEM((2, NSN, 2, listed, BLK, half), jnp.bfloat16),
            pltpu.VMEM(side, jnp.float32),
            pltpu.VMEM(side, jnp.float32),
            pltpu.VMEM(side, jnp.float32),
            pltpu.VMEM((per * 2 * BLK, 4 * BLK), jnp.bfloat16),
            pltpu.VMEM((size, half), jnp.float32),
            pltpu.VMEM((NSN, n, piece, half), jnp.int16), pltpu.VMEM((NSN, n, 1, half), jnp.float32),
            pltpu.VMEM((NSN, n, piece, half), jnp.int16), pltpu.VMEM((NSN, n, 1, half), jnp.float32),
            pltpu.VMEM((NSN, n, piece, half), jnp.int16), pltpu.VMEM((NSN, n, 1, half), jnp.float32),
            pltpu.VMEM((NSN, piece, half), jnp.bfloat16),
            dma((blocks_col,)), dma((NSN,)), dma((NSN,)), dma((NSN, nz + 2)), dma((NSN, nz)),
            dma((NSN, nz)), dma((NSN, nz)), dma((NSN, n)), dma((NSN, n)),
            dma((NSN, blocks_row)), dma((NSN, blocks_row)), dma((NSN, blocks_row)),
            dma((NSN, n)), dma((NSN, n)), dma((NSN, n)), dma((NSN, n)),
            dma((NSN, n)), dma((NSN, n)), dma((NSN, n)), dma((NSN, n)),
        ],
        compiler_params=pltpu.CompilerParams(
            collective_id=0, has_side_effects=True, vmem_limit_bytes=66000000),
        name="inversion_step",
    )(row_lists, order, row_lists, order, shards, inverse_pairs, diag_blocks.reshape(size, half))
    return (values, schur.reshape(diag_blocks.shape))


def solution(mesh):
    in_specs = (
        P("pole", "row", "col"),
        P("pole", None, "row", "col"),
        P("pole", None, None, "col"),
        P(),
        P(),
    )
    out_specs = (P("pole", None, "row", "col"), P("pole", None, None, "col"))
    return jax.shard_map(functools.partial(local, mesh.shape["row"]), mesh=mesh, in_specs=in_specs,
                         out_specs=out_specs, check_vma=False)
```

```python
import functools

import jax
import jax.numpy as jnp
from jax import lax
from jax.experimental import pallas as pl
from jax.experimental.pallas import tpu as pltpu
from jax.sharding import PartitionSpec as P

NSN = 2
BLK = 128
MESH = pl.DeviceIdType.MESH
ANY = pl.BlockSpec(memory_space=pl.ANY)
VMEM = pl.BlockSpec(memory_space=pltpu.VMEM)
SMEM = pl.BlockSpec(memory_space=pltpu.SMEM)


def aligned(start, size):
    return pl.ds(pl.multiple_of(start, size), size)


def index_tables(lists_s, order_s, lists_v, order_v, pick, keep, local_pick, local_keep, first, row, blocks_col, blocks_row):
    order = order_v[...]
    storage = lax.broadcasted_iota(jnp.int32, order.shape, 1)
    for k in range(lists_s.shape[0]):
        for j in range(lists_s.shape[1]):
            at = jnp.sum(jnp.where(order == lists_s[k, j], storage, 0)) - first
            inside = (at >= 0) & (at < blocks_col)
            pick[k, j] = jnp.clip(at, 0, blocks_col - 1)
            keep[k, j] = jnp.where(inside, 1.0, 0.0)
        listed = lists_v[k:k + 1, :]
        entry = lax.broadcasted_iota(jnp.int32, listed.shape, 1) + 1
        for t in range(blocks_row):
            found = jnp.sum(jnp.where(listed == order_s[0, row * blocks_row + t], entry, 0))
            local_pick[k, t] = jnp.clip(found - 1, 0, lists_s.shape[1] - 1)
            local_keep[k, t] = jnp.where(found > 0, 1.0, 0.0)


def coded(value):
    most = jnp.maximum(jnp.max(jnp.abs(value), axis=0, keepdims=True), 1e-33)
    return jnp.round(value * (32767.0 / most)).astype(jnp.int32).astype(jnp.int16), most * (1.0 / 32767.0)


def decoded(code, scale):
    return code.astype(jnp.int32).astype(jnp.float32) * scale


def kernel(n, ny, lists_s, order_s, lists_v, order_v, x_ref, a_ref, diag_ref, own, sum_ref,
           pick, keep, local_pick, local_keep, a_buf, g_ref, oth, recv, bbuf, mine, codes, scales, got_codes, got_scales, all_codes, all_scales, diag,
           a_sem, loc_sem, diag_sem, z_send, z_recv, y_send, y_recv, s_send, s_recv,
           v_send, v_recv, o_sem, r_send, r_recv, rs_send, rs_recv, b_send, b_recv, bs_send, bs_recv):
    nz = n // ny
    span = g_ref.shape[3] * BLK // n
    rows = a_ref.shape[1]
    blocks_col = a_ref.shape[2] // BLK
    blocks_row = rows // BLK
    tile = rows if rows <= 1536 else BLK
    per = max(1, span // BLK)
    unit = min(span, BLK)
    row = lax.axis_index("row")
    col = lax.axis_index("col")
    z = row // ny
    y = row % ny
    oy = ny - 1 - y
    sibling = {"col": 1 - col}
    up = {"row": row + ny}
    down = {"row": row - ny}
    across = {"row": z * ny + oy}
    size = sum_ref.shape[0] // (NSN * n)

    def place(k, r):
        return aligned(k * n * size + r * size, size)

    def stream(b):
        return pltpu.make_async_copy(a_ref.at[:, :, aligned(b * BLK, BLK)], a_buf.at[b], a_sem.at[b])

    def start_stream(b, carry):
        stream(b).start()
        return carry

    def wait_stream(b, carry):
        stream(b).wait()
        return carry

    def slot(c, k, r):
        if span >= BLK:
            return g_ref.at[c, k, :, pl.ds(r * per, per)]
        return g_ref.at[c, k, :, r * span // BLK, aligned(r * span % BLK, span)]

    def local(k):
        return pltpu.make_async_copy(x_ref.at[k], slot(col, k, row), loc_sem.at[k])

    def own_diag(k):
        return pltpu.make_async_copy(diag_ref.at[place(k, row)], diag.at[k], diag_sem.at[k])

    for k in range(NSN):
        local(k).start()
    lax.fori_loop(0, blocks_col, start_stream, 0)

    barrier = pltpu.get_barrier_semaphore()
    pl.semaphore_signal(barrier, inc=1, device_id=sibling, device_id_type=MESH)
    for d in range(1, n):
        pl.semaphore_signal(barrier, inc=1, device_id={"row": (row + d) % n}, device_id_type=MESH)
    pl.semaphore_wait(barrier, n)

    def copy(src, c, k, r, send, got, target):
        return pltpu.make_async_remote_copy(
            src_ref=src, dst_ref=slot(c, k, r), send_sem=send, recv_sem=got,
            device_id=target, device_id_type=MESH)

    def line(src, k, zz, target):
        return copy(src, col, k, zz * ny + y, z_send.at[k, zz], z_recv.at[k, zz], target)

    def side(src, k, zz, yy):
        return copy(src, col, k, zz * ny + yy, y_send.at[k, zz], y_recv.at[k, zz], across)

    def sib(src, c, k, r):
        return copy(src, c, k, r, s_send.at[k, r], s_recv.at[k, r], sibling)

    def here(k, zz, yy):
        return slot(col, k, zz * ny + yy)

    def first_up(k):
        return copy(x_ref.at[k], col, k, row, z_send.at[k, nz], z_recv.at[k, z], up)

    def first_down(k):
        return copy(x_ref.at[k], col, k, row, z_send.at[k, nz + 1], z_recv.at[k, z], down)

    for k in range(NSN):
        side(x_ref.at[k], k, z, y).start()
        pl.when(z < nz - 1)(lambda k=k: first_up(k).start())
        pl.when(z > 0)(lambda k=k: first_down(k).start())
        sib(x_ref.at[k], col, k, row).start()
    for k in range(NSN):
        own_diag(k).start()
    index_tables(lists_s, order_s, lists_v, order_v, pick, keep, local_pick, local_keep,
                 col * blocks_col, row, blocks_col, blocks_row)
    own[...] = jnp.zeros_like(own)
    oth[...] = jnp.zeros_like(oth)
    mine[...] = jnp.zeros_like(mine)
    for k in range(NSN):
        local(k).wait()

    def from_line(k, zz, forward, target):
        line(here(k, zz, y), k, zz, target).wait_recv()

        @pl.when(forward)
        def _():
            line(here(k, zz, y), k, zz, target).start()

        side(here(k, zz, y), k, zz, y).start()
        sib(here(k, zz, y), col, k, zz * ny + y).start()

    def from_side(k, zz):
        side(here(k, zz, oy), k, zz, oy).wait_recv()
        sib(here(k, zz, oy), col, k, zz * ny + oy).start()

    outs = (own, oth)

    def multiply(k, r):
        sib(slot(1 - col, k, r), 1 - col, k, r).wait_recv()
        if unit < BLK:
            bbuf[...] = jnp.zeros_like(bbuf)
        for e in range(per):
            start = r * span + e * BLK
            scale = keep[k, start // BLK]
            base = e * 2 * BLK
            if unit < BLK:
                shift = start % BLK
                top = aligned(base + shift, unit)
                low = aligned(base + BLK + shift, unit)
            else:
                top = pl.ds(base, unit)
                low = pl.ds(base + BLK, unit)
            for rel in range(2):
                c = col if rel == 0 else 1 - col
                at = pl.ds(0, unit) if unit == BLK else aligned(start % BLK, unit)
                real = (g_ref[c, k, 0, start // BLK, at, :].astype(jnp.float32) * scale).astype(jnp.bfloat16)
                imag = (g_ref[c, k, 1, start // BLK, at, :].astype(jnp.float32) * scale).astype(jnp.bfloat16)
                left = rel * 2 * BLK
                bbuf[top, left:left + BLK] = -real
                bbuf[top, left + BLK:left + 2 * BLK] = -imag
                bbuf[low, left:left + BLK] = imag
                bbuf[low, left + BLK:left + 2 * BLK] = -real

        def by_tile(t, inner):
            at = aligned(t * tile, tile)
            pieces = []
            for e in range(per):
                block = pick[k, (r * span + e * BLK) // BLK]
                pieces += [a_buf[block, 0, at, :], a_buf[block, 1, at, :]]
            left = jnp.concatenate(pieces, axis=1)
            for rel in range(2):
                found = jnp.dot(left, bbuf[:, rel * 2 * BLK:(rel + 1) * 2 * BLK],
                                preferred_element_type=jnp.float32)
                outs[rel][k, 0, at, :] += found[:, :BLK]
                outs[rel][k, 1, at, :] += found[:, BLK:]
            return inner

        lax.fori_loop(0, rows // tile, by_tile, 0)

    group = 3 if blocks_row % 3 == 0 else 1
    strips = blocks_row // group
    high = group * BLK

    def strip(k, s):
        return k, slice(None), aligned(s * high, high)

    def swap(k, s):
        return pltpu.make_async_remote_copy(
            src_ref=oth.at[strip(k, s)], dst_ref=recv.at[strip(k, s)], send_sem=v_send.at[k, s], recv_sem=v_recv.at[k, s],
            device_id=sibling, device_id_type=MESH)

    def start_swaps(k):
        def one(s, carry):
            swap(k, s).start()
            return carry
        lax.fori_loop(0, strips, one, 0)


    steps = 2 * nz
    last = NSN + 4 * (steps - 1)

    def entry(e, carry):
        pl.when(e == last)(lambda: start_swaps(0))
        g = (e - NSN) // 4
        q = (e - NSN) % 4
        away = g // 2 + 1 - q // 2
        mine_first = e < NSN
        k = jnp.where(mine_first, e, g % 2)
        zz = z + jnp.where(mine_first, 0, jnp.where(q % 2 == 0, -away, away))
        yy = jnp.where(mine_first | (q // 2 == 0), y, oy)
        valid = mine_first | ((zz >= 0) & (zz < nz) & ((away > 0) | (q % 2 == 0)))
        pl.when(valid)(lambda: multiply(k, zz * ny + yy))
        return carry

    def done_by(m):
        lag = jnp.where(m >= steps - 2, 0, jnp.where(m < 4, 2, 1))
        return jnp.where(m < 1, 0, NSN + 4 * jnp.maximum(m - lag + 1, 0))

    def step(m, carry):
        d = m // 2 + 1
        k = m % 2
        pl.when(z - d >= 0)(lambda: from_line(k, z - d, z < nz - 1, up))
        pl.when(z + d < nz)(lambda: from_line(k, z + d, z > 0, down))
        pl.when(z - d + 1 >= 0)(lambda: from_side(k, z - d + 1))
        pl.when((d > 1) & (z + d - 1 < nz))(lambda: from_side(k, z + d - 1))
        pl.when(m == 1)(lambda: lax.fori_loop(0, blocks_col, wait_stream, None))
        lax.fori_loop(done_by(m - 1), done_by(m), entry, 0)
        return carry

    lax.fori_loop(0, steps, step, 0)
    start_swaps(1)

    def scatter(k, d):
        to = (row + d) % n
        code = pltpu.make_async_remote_copy(
            src_ref=codes.at[k, to], dst_ref=got_codes.at[k, d],
            send_sem=r_send.at[k, d], recv_sem=r_recv.at[k, d],
            device_id={"row": to}, device_id_type=MESH)
        scale = pltpu.make_async_remote_copy(
            src_ref=scales.at[k, to], dst_ref=got_scales.at[k, d],
            send_sem=rs_send.at[k, d], recv_sem=rs_recv.at[k, d],
            device_id={"row": to}, device_id_type=MESH)
        return code, scale

    def spread(k, d, owner):
        to = (row + d) % n
        code = pltpu.make_async_remote_copy(
            src_ref=all_codes.at[k, owner], dst_ref=all_codes.at[k, owner],
            send_sem=b_send.at[k, d], recv_sem=b_recv.at[k, d],
            device_id={"row": to}, device_id_type=MESH)
        scale = pltpu.make_async_remote_copy(
            src_ref=all_scales.at[k, owner], dst_ref=all_scales.at[k, owner],
            send_sem=bs_send.at[k, d], recv_sem=bs_recv.at[k, d],
            device_id={"row": to}, device_id_type=MESH)
        return code, scale

    width = 2 * BLK
    for k in range(NSN):
        def correct(s, carry, k=k):
            swap(k, s).wait_recv()
            own[strip(k, s)] += recv[strip(k, s)]
            left, right = [], []
            for u in range(group):
                t = s * group + u
                j = local_pick[k, t]
                scale = local_keep[k, t]
                for p in range(2):
                    left.append(jnp.concatenate([g_ref[0, k, p, j], g_ref[1, k, p, j]], axis=1))
                real = own[k, 0, aligned(t * BLK, BLK), :] * scale
                imag = own[k, 1, aligned(t * BLK, BLK), :] * scale
                right.append(jnp.concatenate([real, imag], axis=1))
                right.append(jnp.concatenate([-imag, real], axis=1))
            factor = jnp.concatenate(left, axis=0)
            wide = jnp.concatenate(right, axis=0)
            total = None
            for _ in range(2):
                piece = wide.astype(jnp.bfloat16)
                wide = wide - piece.astype(jnp.float32)
                term = lax.dot_general(factor, piece, (((0,), (0,)), ((), ())),
                                       preferred_element_type=jnp.float32)
                total = term if total is None else total + term
            mine[2 * k * width:(2 * k + 1) * width, :] += total[:, :BLK]
            mine[(2 * k + 1) * width:(2 * k + 2) * width, :] += total[:, BLK:]
            return carry

        lax.fori_loop(0, strips, correct, 0)

        def encode(r, carry, k=k):
            codes[k, r], scales[k, r] = coded(mine[place(k, r), :])
            return carry

        lax.fori_loop(0, n, encode, 0)
        for d in range(1, n):
            for c in scatter(k, d):
                c.start()

    for k in range(NSN):
        own_diag(k).wait()
        total = mine[place(k, row), :]
        for d in range(1, n):
            for c in scatter(k, d):
                c.wait_recv()
            total = total + decoded(got_codes[k, d], got_scales[k, d])
        all_codes[k, row], all_scales[k, row] = coded(diag[k].astype(jnp.float32) - total)
        for d in range(1, n):
            for c in spread(k, d, row):
                c.start()

    for k in range(NSN):
        for r in range(n):
            sib(slot(col, k, r), col, k, r).wait_send()
        for zz in range(nz):
            side(here(k, zz, y), k, zz, y).wait_send()
            pl.when(((zz < z) & (z < nz - 1)) | ((zz > z) & (z > 0)))(
                lambda k=k, zz=zz: line(here(k, zz, y), k, zz, up).wait_send())
        pl.when(z < nz - 1)(lambda k=k: first_up(k).wait_send())
        pl.when(z > 0)(lambda k=k: first_down(k).wait_send())
        def drain(s, carry, k=k):
            swap(k, s).wait_send()
            return carry

        lax.fori_loop(0, strips, drain, 0)
        for d in range(1, n):
            for c in scatter(k, d) + spread(k, d, row):
                c.wait_send()

    for k in range(NSN):
        for d in range(1, n):
            for c in spread(k, d, (row - d) % n):
                c.wait_recv()

        def decode(r, carry, k=k):
            sum_ref[place(k, r), :] = decoded(all_codes[k, r], all_scales[k, r])
            return carry

        lax.fori_loop(0, n, decode, 0)


def local(n, inverse_pairs, factor_rows, diag_blocks, row_lists, block_order):
    rows, cols = inverse_pairs.shape[1:]
    blocks_row, blocks_col = rows // BLK, cols // BLK
    listed = row_lists.shape[1]
    order = block_order.reshape(1, -1)

    ny = 2 if n % 2 == 0 else 1
    nz = n // ny
    span, half = factor_rows.shape[2:]
    size = NSN * 2 * 2 * half
    piece = size // (NSN * n)
    per = max(1, span // BLK)
    shards = factor_rows.reshape(NSN, 2, per, BLK, half) if span >= BLK else factor_rows
    dma = pltpu.SemaphoreType.DMA
    side = (NSN, 2, rows, half)
    values, schur = pl.pallas_call(
        functools.partial(kernel, n, ny),
        out_shape=(pltpu.VMEM(side, jnp.float32), pltpu.VMEM((size, half), jnp.float32)),
        in_specs=[SMEM, SMEM, VMEM, VMEM, ANY, ANY, ANY],
        out_specs=(VMEM, VMEM),
        scratch_shapes=[
            pltpu.SMEM((NSN, listed), jnp.int32),
            pltpu.SMEM((NSN, listed), jnp.float32),
            pltpu.SMEM((NSN, blocks_row), jnp.int32),
            pltpu.SMEM((NSN, blocks_row), jnp.float32),
            pltpu.VMEM((blocks_col, 2, rows, BLK), jnp.bfloat16),
            pltpu.VMEM((2, NSN, 2, listed, BLK, half), jnp.bfloat16),
            pltpu.VMEM(side, jnp.float32),
            pltpu.VMEM(side, jnp.float32),
            pltpu.VMEM((per * 2 * BLK, 4 * BLK), jnp.bfloat16),
            pltpu.VMEM((size, half), jnp.float32),
            pltpu.VMEM((NSN, n, piece, half), jnp.int16), pltpu.VMEM((NSN, n, 1, half), jnp.float32),
            pltpu.VMEM((NSN, n, piece, half), jnp.int16), pltpu.VMEM((NSN, n, 1, half), jnp.float32),
            pltpu.VMEM((NSN, n, piece, half), jnp.int16), pltpu.VMEM((NSN, n, 1, half), jnp.float32),
            pltpu.VMEM((NSN, piece, half), jnp.bfloat16),
            dma((blocks_col,)), dma((NSN,)), dma((NSN,)), dma((NSN, nz + 2)), dma((NSN, nz)),
            dma((NSN, nz)), dma((NSN, nz)), dma((NSN, n)), dma((NSN, n)),
            dma((NSN, blocks_row)), dma((NSN, blocks_row)), dma((NSN, blocks_row)),
            dma((NSN, n)), dma((NSN, n)), dma((NSN, n)), dma((NSN, n)),
            dma((NSN, n)), dma((NSN, n)), dma((NSN, n)), dma((NSN, n)),
        ],
        compiler_params=pltpu.CompilerParams(
            collective_id=0, has_side_effects=True, vmem_limit_bytes=58000000),
        name="inversion_step",
    )(row_lists, order, row_lists, order, shards, inverse_pairs, diag_blocks.reshape(size, half))
    return (values, schur.reshape(diag_blocks.shape))


def solution(mesh):
    in_specs = (
        P("pole", "row", "col"),
        P("pole", None, "row", "col"),
        P("pole", None, None, "col"),
        P(),
        P(),
    )
    out_specs = (P("pole", None, "row", "col"), P("pole", None, None, "col"))
    return jax.shard_map(functools.partial(local, mesh.shape["row"]), mesh=mesh, in_specs=in_specs,
                         out_specs=out_specs, check_vma=False)
```

```python
import functools

import jax
import jax.numpy as jnp
from jax import lax
from jax.experimental import pallas as pl
from jax.experimental.pallas import tpu as pltpu
from jax.sharding import PartitionSpec as P

NSN = 2
BLK = 128
MESH = pl.DeviceIdType.MESH
ANY = pl.BlockSpec(memory_space=pl.ANY)
VMEM = pl.BlockSpec(memory_space=pltpu.VMEM)
SMEM = pl.BlockSpec(memory_space=pltpu.SMEM)


def aligned(start, size):
    return pl.ds(pl.multiple_of(start, size), size)


def index_tables(lists_s, order_s, lists_v, order_v, pick, keep, local_pick, local_keep, first, row, blocks_col, blocks_row):
    order = order_v[...]
    storage = lax.broadcasted_iota(jnp.int32, order.shape, 1)
    for k in range(lists_s.shape[0]):
        for j in range(lists_s.shape[1]):
            at = jnp.sum(jnp.where(order == lists_s[k, j], storage, 0)) - first
            inside = (at >= 0) & (at < blocks_col)
            pick[k, j] = jnp.clip(at, 0, blocks_col - 1)
            keep[k, j] = jnp.where(inside, 1.0, 0.0)
        listed = lists_v[k:k + 1, :]
        entry = lax.broadcasted_iota(jnp.int32, listed.shape, 1) + 1
        for t in range(blocks_row):
            found = jnp.sum(jnp.where(listed == order_s[0, row * blocks_row + t], entry, 0))
            local_pick[k, t] = jnp.clip(found - 1, 0, lists_s.shape[1] - 1)
            local_keep[k, t] = jnp.where(found > 0, 1.0, 0.0)


def coded(value):
    most = jnp.maximum(jnp.max(jnp.abs(value), axis=-2, keepdims=True), 1e-33)
    return jnp.round(value * (32767.0 / most)).astype(jnp.int32).astype(jnp.int16), most * (1.0 / 32767.0)


def decoded(code, scale):
    return code.astype(jnp.int32).astype(jnp.float32) * scale


def kernel(n, ny, lists_s, order_s, lists_v, order_v, x_ref, a_ref, diag_ref, own, sum_ref,
           pick, keep, local_pick, local_keep, a_top, a_low, g_ref, oth, recv, bbuf, mine, codes, scales, got_codes, got_scales, all_codes, all_scales, diag,
           a_sem, loc_sem, diag_sem, z_send, z_recv, y_send, y_recv, s_send, s_recv,
           v_send, v_recv, o_sem, r_send, r_recv, rs_send, rs_recv, b_send, b_recv, bs_send, bs_recv):
    nz = n // ny
    span = g_ref.shape[3] * BLK // n
    rows = a_ref.shape[1]
    blocks_col = a_ref.shape[2] // BLK
    blocks_row = rows // BLK
    tall = a_top.shape[2]
    per = max(1, span // BLK)
    unit = min(span, BLK)
    row = lax.axis_index("row")
    col = lax.axis_index("col")
    z = row // ny
    y = row % ny
    oy = ny - 1 - y
    sibling = {"col": 1 - col}
    up = {"row": row + ny}
    down = {"row": row - ny}
    across = {"row": z * ny + oy}
    size = sum_ref.shape[0] // (NSN * n)

    def place(k, r):
        return aligned(k * n * size + r * size, size)

    def stream(half, b):
        a_half = a_low if half else a_top
        return pltpu.make_async_copy(
            a_ref.at[:, half * tall:(half + 1) * tall, aligned(b * BLK, BLK)], a_half.at[b], a_sem.at[half, b])

    def start_stream(half):
        def one(b, carry):
            stream(half, b).start()
            return carry
        lax.fori_loop(0, blocks_col, one, 0)

    def wait_stream(half):
        def one(b, carry):
            stream(half, b).wait()
            return carry
        lax.fori_loop(0, blocks_col, one, 0)

    def slot(c, k, r):
        if span >= BLK:
            return g_ref.at[c, k, :, pl.ds(r * per, per)]
        return g_ref.at[c, k, :, r * span // BLK, aligned(r * span % BLK, span)]

    def local(k):
        return pltpu.make_async_copy(x_ref.at[k], slot(col, k, row), loc_sem.at[k])

    def own_diag(k):
        return pltpu.make_async_copy(diag_ref.at[place(k, row)], diag.at[k], diag_sem.at[k])

    for k in range(NSN):
        local(k).start()
    for half in range(2):
        start_stream(half)

    barrier = pltpu.get_barrier_semaphore()
    pl.semaphore_signal(barrier, inc=1, device_id=sibling, device_id_type=MESH)
    pl.semaphore_signal(barrier, inc=1, device_id=across, device_id_type=MESH)
    pl.when(z < nz - 1)(lambda: pl.semaphore_signal(barrier, inc=1, device_id=up, device_id_type=MESH))
    pl.when(z > 0)(lambda: pl.semaphore_signal(barrier, inc=1, device_id=down, device_id_type=MESH))
    pl.semaphore_wait(barrier, 2 + jnp.where(z < nz - 1, 1, 0) + jnp.where(z > 0, 1, 0))

    def copy(src, c, k, r, send, got, target):
        return pltpu.make_async_remote_copy(
            src_ref=src, dst_ref=slot(c, k, r), send_sem=send, recv_sem=got,
            device_id=target, device_id_type=MESH)

    def line(src, k, zz, target):
        return copy(src, col, k, zz * ny + y, z_send.at[k, zz], z_recv.at[k, zz], target)

    def side(src, k, zz, yy):
        return copy(src, col, k, zz * ny + yy, y_send.at[k, zz], y_recv.at[k, zz], across)

    def sib(src, c, k, r):
        return copy(src, c, k, r, s_send.at[k, r], s_recv.at[k, r], sibling)

    def here(k, zz, yy):
        return slot(col, k, zz * ny + yy)

    def first_up(k):
        return copy(x_ref.at[k], col, k, row, z_send.at[k, nz], z_recv.at[k, z], up)

    def first_down(k):
        return copy(x_ref.at[k], col, k, row, z_send.at[k, nz + 1], z_recv.at[k, z], down)

    for k in range(NSN):
        side(x_ref.at[k], k, z, y).start()
        pl.when(z < nz - 1)(lambda k=k: first_up(k).start())
        pl.when(z > 0)(lambda k=k: first_down(k).start())
        sib(x_ref.at[k], col, k, row).start()
    for k in range(NSN):
        own_diag(k).start()
    index_tables(lists_s, order_s, lists_v, order_v, pick, keep, local_pick, local_keep,
                 col * blocks_col, row, blocks_col, blocks_row)
    own[...] = jnp.zeros_like(own)
    oth[...] = jnp.zeros_like(oth)
    mine[...] = jnp.zeros_like(mine)
    for k in range(NSN):
        local(k).wait()

    def from_line(k, zz, forward, target):
        line(here(k, zz, y), k, zz, target).wait_recv()

        @pl.when(forward)
        def _():
            line(here(k, zz, y), k, zz, target).start()

        side(here(k, zz, y), k, zz, y).start()
        sib(here(k, zz, y), col, k, zz * ny + y).start()

    def from_side(k, zz):
        side(here(k, zz, oy), k, zz, oy).wait_recv()
        sib(here(k, zz, oy), col, k, zz * ny + oy).start()

    outs = (own, oth)

    def multiply(k, r, halves, fresh):
        if fresh:
            sib(slot(1 - col, k, r), 1 - col, k, r).wait_recv()
        if unit < BLK:
            bbuf[...] = jnp.zeros_like(bbuf)
        for e in range(per):
            start = r * span + e * BLK
            scale = keep[k, start // BLK]
            base = e * 2 * BLK
            if unit < BLK:
                shift = start % BLK
                top = aligned(base + shift, unit)
                low = aligned(base + BLK + shift, unit)
            else:
                top = pl.ds(base, unit)
                low = pl.ds(base + BLK, unit)
            for rel in range(2):
                c = col if rel == 0 else 1 - col
                at = pl.ds(0, unit) if unit == BLK else aligned(start % BLK, unit)
                real = (g_ref[c, k, 0, start // BLK, at, :].astype(jnp.float32) * scale).astype(jnp.bfloat16)
                imag = (g_ref[c, k, 1, start // BLK, at, :].astype(jnp.float32) * scale).astype(jnp.bfloat16)
                left = rel * 2 * BLK
                bbuf[top, left:left + BLK] = -real
                bbuf[top, left + BLK:left + 2 * BLK] = -imag
                bbuf[low, left:left + BLK] = imag
                bbuf[low, left + BLK:left + 2 * BLK] = -real

        at = slice(halves[0] * tall, (halves[-1] + 1) * tall)
        left = []
        for half in halves:
            a_half = a_low if half else a_top
            pieces = []
            for e in range(per):
                block = pick[k, (r * span + e * BLK) // BLK]
                pieces += [a_half[block, 0], a_half[block, 1]]
            left.append(jnp.concatenate(pieces, axis=1))
        left = jnp.concatenate(left, axis=0) if len(left) > 1 else left[0]
        for rel in range(2):
            found = jnp.dot(left, bbuf[:, rel * 2 * BLK:(rel + 1) * 2 * BLK],
                            preferred_element_type=jnp.float32)
            outs[rel][k, 0, at, :] += found[:, :BLK]
            outs[rel][k, 1, at, :] += found[:, BLK:]

    group = 3 if blocks_row % 3 == 0 else 1
    strips = blocks_row // group
    high = group * BLK

    def strip(k, s):
        return k, slice(None), aligned(s * high, high)

    def swap(k, s):
        return pltpu.make_async_remote_copy(
            src_ref=oth.at[strip(k, s)], dst_ref=recv.at[strip(k, s)], send_sem=v_send.at[k, s], recv_sem=v_recv.at[k, s],
            device_id=sibling, device_id_type=MESH)

    def start_swaps(k):
        def one(s, carry):
            swap(k, s).start()
            return carry
        lax.fori_loop(0, strips, one, 0)


    steps = max(2 * nz, 4)
    last = NSN + 4 * (steps - 1)

    def entries(low, high, halves, fresh):
        def entry(e, carry):
            if len(halves) > 1:
                pl.when(e == last)(lambda: start_swaps(0))
            g = (e - NSN) // 4
            q = (e - NSN) % 4
            away = g // 2 + 1 - q // 2
            mine_first = e < NSN
            k = jnp.where(mine_first, e, g % 2)
            zz = z + jnp.where(mine_first, 0, jnp.where(q % 2 == 0, -away, away))
            yy = jnp.where(mine_first | (q // 2 == 0), y, oy)
            valid = mine_first | ((zz >= 0) & (zz < nz) & ((away > 0) | (q % 2 == 0)))
            pl.when(valid)(lambda: multiply(k, zz * ny + yy, halves, fresh))
            return carry

        lax.fori_loop(low, high, entry, 0)

    def done_by(m):
        ahead = NSN + 4 * jnp.where(m >= steps - 2, m + 1, m)
        return jnp.where(m < 3, NSN + 8, NSN + 4 * jnp.where(m >= steps - 1, m + 1, m))

    def step(m, carry):
        d = m // 2 + 1
        k = m % 2
        pl.when(z - d >= 0)(lambda: from_line(k, z - d, z < nz - 1, up))
        pl.when(z + d < nz)(lambda: from_line(k, z + d, z > 0, down))
        pl.when(z - d + 1 >= 0)(lambda: from_side(k, z - d + 1))
        pl.when((d > 1) & (z + d - 1 < nz))(lambda: from_side(k, z + d - 1))
        pl.when(m == 0)(lambda: wait_stream(0))
        pl.when(m == 2)(lambda: wait_stream(1))
        cut = NSN + 4
        low, high = jnp.where(m % 2 == 0, 0, cut), jnp.where(m % 2 == 0, cut, cut + 4)
        pl.when(m < 2)(lambda: entries(low, high, (0,), True))
        pl.when((m >= 2) & (m < 4))(lambda: entries(low, high, (1,), False))
        entries(done_by(m - 1), done_by(m), (0, 1), True)
        return carry

    lax.fori_loop(0, steps, step, 0)
    start_swaps(1)

    def scatter(k, d):
        to = (row + d) % n
        code = pltpu.make_async_remote_copy(
            src_ref=codes.at[k, to], dst_ref=got_codes.at[k, d],
            send_sem=r_send.at[k, d], recv_sem=r_recv.at[k, d],
            device_id={"row": to}, device_id_type=MESH)
        scale = pltpu.make_async_remote_copy(
            src_ref=scales.at[k, to], dst_ref=got_scales.at[k, d],
            send_sem=rs_send.at[k, d], recv_sem=rs_recv.at[k, d],
            device_id={"row": to}, device_id_type=MESH)
        return code, scale

    def spread(k, d, owner):
        to = (row + d) % n
        code = pltpu.make_async_remote_copy(
            src_ref=all_codes.at[k, owner], dst_ref=all_codes.at[k, owner],
            send_sem=b_send.at[k, d], recv_sem=b_recv.at[k, d],
            device_id={"row": to}, device_id_type=MESH)
        scale = pltpu.make_async_remote_copy(
            src_ref=all_scales.at[k, owner], dst_ref=all_scales.at[k, owner],
            send_sem=bs_send.at[k, d], recv_sem=bs_recv.at[k, d],
            device_id={"row": to}, device_id_type=MESH)
        return code, scale

    width = 2 * BLK
    for k in range(NSN):
        def correct(s, carry, k=k):
            swap(k, s).wait_recv()
            own[strip(k, s)] += recv[strip(k, s)]
            left, right = [], []
            for u in range(group):
                t = s * group + u
                j = local_pick[k, t]
                scale = local_keep[k, t]
                for p in range(2):
                    left.append(jnp.concatenate([g_ref[0, k, p, j], g_ref[1, k, p, j]], axis=1))
                real = own[k, 0, aligned(t * BLK, BLK), :] * scale
                imag = own[k, 1, aligned(t * BLK, BLK), :] * scale
                right.append(jnp.concatenate([real, imag], axis=1))
                right.append(jnp.concatenate([-imag, real], axis=1))
            factor = jnp.concatenate(left, axis=0)
            wide = jnp.concatenate(right, axis=0)
            total = None
            for _ in range(2):
                piece = wide.astype(jnp.bfloat16)
                wide = wide - piece.astype(jnp.float32)
                term = lax.dot_general(factor, piece, (((0,), (0,)), ((), ())),
                                       preferred_element_type=jnp.float32)
                total = term if total is None else total + term
            mine[2 * k * width:(2 * k + 1) * width, :] += total[:, :BLK]
            mine[(2 * k + 1) * width:(2 * k + 2) * width, :] += total[:, BLK:]
            return carry

        lax.fori_loop(0, strips, correct, 0)

        codes[k], scales[k] = coded(mine[k * n * size:(k + 1) * n * size, :].reshape(codes.shape[1:]))
        for d in range(1, n):
            for c in scatter(k, d):
                c.start()

    for k in range(NSN):
        own_diag(k).wait()
        total = mine[place(k, row), :]
        for d in range(1, n):
            for c in scatter(k, d):
                c.wait_recv()
            total = total + decoded(got_codes[k, d], got_scales[k, d])
        all_codes[k, row], all_scales[k, row] = coded(diag[k].astype(jnp.float32) - total)
        for d in range(1, n):
            for c in spread(k, d, row):
                c.start()

    for k in range(NSN):
        for r in range(n):
            sib(slot(col, k, r), col, k, r).wait_send()
        for zz in range(nz):
            side(here(k, zz, y), k, zz, y).wait_send()
            pl.when(((zz < z) & (z < nz - 1)) | ((zz > z) & (z > 0)))(
                lambda k=k, zz=zz: line(here(k, zz, y), k, zz, up).wait_send())
        pl.when(z < nz - 1)(lambda k=k: first_up(k).wait_send())
        pl.when(z > 0)(lambda k=k: first_down(k).wait_send())
        def drain(s, carry, k=k):
            swap(k, s).wait_send()
            return carry

        lax.fori_loop(0, strips, drain, 0)
        for d in range(1, n):
            for c in scatter(k, d) + spread(k, d, row):
                c.wait_send()

    for k in range(NSN):
        for d in range(1, n):
            for c in spread(k, d, (row - d) % n):
                c.wait_recv()

        sum_ref[k * n * size:(k + 1) * n * size, :] = decoded(all_codes[k], all_scales[k]).reshape(n * size, sum_ref.shape[1])


def local(n, inverse_pairs, factor_rows, diag_blocks, row_lists, block_order):
    rows, cols = inverse_pairs.shape[1:]
    blocks_row, blocks_col = rows // BLK, cols // BLK
    listed = row_lists.shape[1]
    order = block_order.reshape(1, -1)

    ny = 2 if n % 2 == 0 else 1
    nz = n // ny
    span, half = factor_rows.shape[2:]
    size = NSN * 2 * 2 * half
    piece = size // (NSN * n)
    per = max(1, span // BLK)
    shards = factor_rows.reshape(NSN, 2, per, BLK, half) if span >= BLK else factor_rows
    dma = pltpu.SemaphoreType.DMA
    side = (NSN, 2, rows, half)
    values, schur = pl.pallas_call(
        functools.partial(kernel, n, ny),
        out_shape=(pltpu.VMEM(side, jnp.float32), pltpu.VMEM((size, half), jnp.float32)),
        in_specs=[SMEM, SMEM, VMEM, VMEM, ANY, ANY, ANY],
        out_specs=(VMEM, VMEM),
        scratch_shapes=[
            pltpu.SMEM((NSN, listed), jnp.int32),
            pltpu.SMEM((NSN, listed), jnp.float32),
            pltpu.SMEM((NSN, blocks_row), jnp.int32),
            pltpu.SMEM((NSN, blocks_row), jnp.float32),
            pltpu.VMEM((blocks_col, 2, rows // 2, BLK), jnp.bfloat16),
            pltpu.VMEM((blocks_col, 2, rows // 2, BLK), jnp.bfloat16),
            pltpu.VMEM((2, NSN, 2, listed, BLK, half), jnp.bfloat16),
            pltpu.VMEM(side, jnp.float32),
            pltpu.VMEM(side, jnp.float32),
            pltpu.VMEM((per * 2 * BLK, 4 * BLK), jnp.bfloat16),
            pltpu.VMEM((size, half), jnp.float32),
            pltpu.VMEM((NSN, n, piece, half), jnp.int16), pltpu.VMEM((NSN, n, 1, half), jnp.float32),
            pltpu.VMEM((NSN, n, piece, half), jnp.int16), pltpu.VMEM((NSN, n, 1, half), jnp.float32),
            pltpu.VMEM((NSN, n, piece, half), jnp.int16), pltpu.VMEM((NSN, n, 1, half), jnp.float32),
            pltpu.VMEM((NSN, piece, half), jnp.bfloat16),
            dma((2, blocks_col)), dma((NSN,)), dma((NSN,)), dma((NSN, nz + 2)), dma((NSN, nz)),
            dma((NSN, nz)), dma((NSN, nz)), dma((NSN, n)), dma((NSN, n)),
            dma((NSN, blocks_row)), dma((NSN, blocks_row)), dma((NSN, blocks_row)),
            dma((NSN, n)), dma((NSN, n)), dma((NSN, n)), dma((NSN, n)),
            dma((NSN, n)), dma((NSN, n)), dma((NSN, n)), dma((NSN, n)),
        ],
        compiler_params=pltpu.CompilerParams(
            collective_id=0, has_side_effects=True, vmem_limit_bytes=58000000),
        name="inversion_step",
    )(row_lists, order, row_lists, order, shards, inverse_pairs, diag_blocks.reshape(size, half))
    return (values, schur.reshape(diag_blocks.shape))


def solution(mesh):
    in_specs = (
        P("pole", "row", "col"),
        P("pole", None, "row", "col"),
        P("pole", None, None, "col"),
        P(),
        P(),
    )
    out_specs = (P("pole", None, "row", "col"), P("pole", None, None, "col"))
    return jax.shard_map(functools.partial(local, mesh.shape["row"]), mesh=mesh, in_specs=in_specs,
                         out_specs=out_specs, check_vma=False)
```

```python
import functools

import jax
import jax.numpy as jnp
from jax import lax
from jax.experimental import pallas as pl
from jax.experimental.pallas import tpu as pltpu
from jax.sharding import PartitionSpec as P

NSN = 2
BLK = 128
MESH = pl.DeviceIdType.MESH
ANY = pl.BlockSpec(memory_space=pl.ANY)
VMEM = pl.BlockSpec(memory_space=pltpu.VMEM)
SMEM = pl.BlockSpec(memory_space=pltpu.SMEM)


def aligned(start, size):
    return pl.ds(pl.multiple_of(start, size), size)


def index_tables(lists_s, order_s, lists_v, order_v, pick, keep, local_pick, local_keep, first, row, blocks_col, blocks_row):
    order = order_v[...]
    storage = lax.broadcasted_iota(jnp.int32, order.shape, 1)
    for k in range(lists_s.shape[0]):
        for j in range(lists_s.shape[1]):
            at = jnp.sum(jnp.where(order == lists_s[k, j], storage, 0)) - first
            inside = (at >= 0) & (at < blocks_col)
            pick[k, j] = jnp.clip(at, 0, blocks_col - 1)
            keep[k, j] = jnp.where(inside, 1.0, 0.0)
        listed = lists_v[k:k + 1, :]
        entry = lax.broadcasted_iota(jnp.int32, listed.shape, 1) + 1
        for t in range(blocks_row):
            found = jnp.sum(jnp.where(listed == order_s[0, row * blocks_row + t], entry, 0))
            local_pick[k, t] = jnp.clip(found - 1, 0, lists_s.shape[1] - 1)
            local_keep[k, t] = jnp.where(found > 0, 1.0, 0.0)


def coded(value):
    most = jnp.maximum(jnp.max(jnp.abs(value), axis=-2, keepdims=True), 1e-33)
    return jnp.round(value * (32767.0 / most)).astype(jnp.int32).astype(jnp.int16), most * (1.0 / 32767.0)


def decoded(code, scale):
    return code.astype(jnp.int32).astype(jnp.float32) * scale


def kernel(n, ny, lists_ref, order_ref, x_ref, a_ref, diag_ref, own, sum_ref,
           lists_s, order_s, lists_v, order_v, pick, keep, local_pick, local_keep, a_top, a_low, g_ref, oth, recv, bbuf, mine, codes, scales, got_codes, got_scales, all_codes, all_scales, diag,
           t_sem, a_sem, loc_sem, diag_sem, z_send, z_recv, y_send, y_recv, s_send, s_recv,
           v_send, v_recv, o_sem, r_send, r_recv, rs_send, rs_recv, b_send, b_recv, bs_send, bs_recv):
    nz = n // ny
    span = g_ref.shape[3] * BLK // n
    rows = a_ref.shape[1]
    blocks_col = a_ref.shape[2] // BLK
    blocks_row = rows // BLK
    tall = a_top.shape[1]
    per = max(1, span // BLK)
    unit = min(span, BLK)
    row = lax.axis_index("row")
    col = lax.axis_index("col")
    z = row // ny
    y = row % ny
    oy = ny - 1 - y
    sibling = {"col": 1 - col}
    up = {"row": row + ny}
    down = {"row": row - ny}
    across = {"row": z * ny + oy}
    size = sum_ref.shape[0] // (NSN * n)

    def place(k, r):
        return aligned(k * n * size + r * size, size)

    def stream(half):
        a_half = a_low if half else a_top
        return pltpu.make_async_copy(a_ref.at[:, half * tall:(half + 1) * tall], a_half, a_sem.at[half])

    def slot(c, k, r):
        if span >= BLK:
            return g_ref.at[c, k, :, pl.ds(r * per, per)]
        return g_ref.at[c, k, :, r * span // BLK, aligned(r * span % BLK, span)]

    def local(k):
        return pltpu.make_async_copy(x_ref.at[k], slot(col, k, row), loc_sem.at[k])

    def own_diag(k):
        return pltpu.make_async_copy(diag_ref.at[place(k, row)], diag.at[k], diag_sem.at[k])

    for k in range(NSN):
        local(k).start()
    tables = [pltpu.make_async_copy(*pair, t_sem.at[i]) for i, pair in enumerate(
        ((lists_ref, lists_s), (order_ref, order_s), (lists_ref, lists_v), (order_ref, order_v)))]
    for c in tables:
        c.start()
    for half in range(2):
        stream(half).start()

    barrier = pltpu.get_barrier_semaphore()
    pl.semaphore_signal(barrier, inc=1, device_id=sibling, device_id_type=MESH)
    pl.semaphore_signal(barrier, inc=1, device_id=across, device_id_type=MESH)
    pl.when(z < nz - 1)(lambda: pl.semaphore_signal(barrier, inc=1, device_id=up, device_id_type=MESH))
    pl.when(z > 0)(lambda: pl.semaphore_signal(barrier, inc=1, device_id=down, device_id_type=MESH))
    pl.semaphore_wait(barrier, 2 + jnp.where(z < nz - 1, 1, 0) + jnp.where(z > 0, 1, 0))

    def copy(src, c, k, r, send, got, target):
        return pltpu.make_async_remote_copy(
            src_ref=src, dst_ref=slot(c, k, r), send_sem=send, recv_sem=got,
            device_id=target, device_id_type=MESH)

    def line(src, k, zz, target):
        return copy(src, col, k, zz * ny + y, z_send.at[k, zz], z_recv.at[k, zz], target)

    def side(src, k, zz, yy):
        return copy(src, col, k, zz * ny + yy, y_send.at[k, zz], y_recv.at[k, zz], across)

    def sib(src, c, k, r):
        return copy(src, c, k, r, s_send.at[k, r], s_recv.at[k, r], sibling)

    def here(k, zz, yy):
        return slot(col, k, zz * ny + yy)

    def first_up(k):
        return copy(x_ref.at[k], col, k, row, z_send.at[k, nz], z_recv.at[k, z], up)

    def first_down(k):
        return copy(x_ref.at[k], col, k, row, z_send.at[k, nz + 1], z_recv.at[k, z], down)

    for k in range(NSN):
        side(x_ref.at[k], k, z, y).start()
        pl.when(z < nz - 1)(lambda k=k: first_up(k).start())
        pl.when(z > 0)(lambda k=k: first_down(k).start())
        sib(x_ref.at[k], col, k, row).start()
    for k in range(NSN):
        own_diag(k).start()
    for c in tables:
        c.wait()
    index_tables(lists_s, order_s, lists_v, order_v, pick, keep, local_pick, local_keep,
                 col * blocks_col, row, blocks_col, blocks_row)
    own[...] = jnp.zeros_like(own)
    oth[...] = jnp.zeros_like(oth)
    mine[...] = jnp.zeros_like(mine)
    for k in range(NSN):
        local(k).wait()

    def from_line(k, zz, forward, target):
        line(here(k, zz, y), k, zz, target).wait_recv()

        @pl.when(forward)
        def _():
            line(here(k, zz, y), k, zz, target).start()

        side(here(k, zz, y), k, zz, y).start()
        sib(here(k, zz, y), col, k, zz * ny + y).start()

    def from_side(k, zz):
        side(here(k, zz, oy), k, zz, oy).wait_recv()
        sib(here(k, zz, oy), col, k, zz * ny + oy).start()

    outs = (own, oth)

    def multiply(k, r, halves, fresh):
        if fresh:
            sib(slot(1 - col, k, r), 1 - col, k, r).wait_recv()
        if unit < BLK:
            bbuf[...] = jnp.zeros_like(bbuf)
        for e in range(per):
            start = r * span + e * BLK
            scale = keep[k, start // BLK]
            base = e * 2 * BLK
            if unit < BLK:
                shift = start % BLK
                top = aligned(base + shift, unit)
                low = aligned(base + BLK + shift, unit)
            else:
                top = pl.ds(base, unit)
                low = pl.ds(base + BLK, unit)
            for rel in range(2):
                c = col if rel == 0 else 1 - col
                at = pl.ds(0, unit) if unit == BLK else aligned(start % BLK, unit)
                real = (g_ref[c, k, 0, start // BLK, at, :].astype(jnp.float32) * scale).astype(jnp.bfloat16)
                imag = (g_ref[c, k, 1, start // BLK, at, :].astype(jnp.float32) * scale).astype(jnp.bfloat16)
                left = rel * 2 * BLK
                bbuf[top, left:left + BLK] = -real
                bbuf[top, left + BLK:left + 2 * BLK] = -imag
                bbuf[low, left:left + BLK] = imag
                bbuf[low, left + BLK:left + 2 * BLK] = -real

        at = slice(halves[0] * tall, (halves[-1] + 1) * tall)
        left = []
        for half in halves:
            a_half = a_low if half else a_top
            pieces = []
            for e in range(per):
                block = pl.ds(pick[k, (r * span + e * BLK) // BLK] * BLK, BLK)
                pieces += [a_half[0, :, block], a_half[1, :, block]]
            left.append(jnp.concatenate(pieces, axis=1))
        left = jnp.concatenate(left, axis=0) if len(left) > 1 else left[0]
        for rel in range(2):
            found = jnp.dot(left, bbuf[:, rel * 2 * BLK:(rel + 1) * 2 * BLK],
                            preferred_element_type=jnp.float32)
            outs[rel][k, 0, at, :] += found[:, :BLK]
            outs[rel][k, 1, at, :] += found[:, BLK:]

    group = 3 if blocks_row % 3 == 0 else 1
    strips = blocks_row // group
    high = group * BLK

    def strip(k, s):
        return k, slice(None), aligned(s * high, high)

    def swap(k, s):
        return pltpu.make_async_remote_copy(
            src_ref=oth.at[strip(k, s)], dst_ref=recv.at[strip(k, s)], send_sem=v_send.at[k, s], recv_sem=v_recv.at[k, s],
            device_id=sibling, device_id_type=MESH)

    def start_swaps(k):
        def one(s, carry):
            swap(k, s).start()
            return carry
        lax.fori_loop(0, strips, one, 0)


    steps = max(2 * nz, 4)
    last = NSN + 4 * (steps - 1)

    def entries(low, high, halves, fresh):
        def entry(e, carry):
            if len(halves) > 1:
                pl.when(e == last)(lambda: start_swaps(0))
            g = (e - NSN) // 4
            q = (e - NSN) % 4
            away = g // 2 + 1 - q // 2
            mine_first = e < NSN
            k = jnp.where(mine_first, e, g % 2)
            zz = z + jnp.where(mine_first, 0, jnp.where(q % 2 == 0, -away, away))
            yy = jnp.where(mine_first | (q // 2 == 0), y, oy)
            valid = mine_first | ((zz >= 0) & (zz < nz) & ((away > 0) | (q % 2 == 0)))
            pl.when(valid)(lambda: multiply(k, zz * ny + yy, halves, fresh))
            return carry

        lax.fori_loop(low, high, entry, 0)

    def done_by(m):
        ahead = NSN + 4 * jnp.where(m >= steps - 2, m + 1, m)
        return jnp.where(m < 3, NSN + 8, NSN + 4 * jnp.where(m >= steps - 1, m + 1, m))

    def step(m, carry):
        d = m // 2 + 1
        k = m % 2
        pl.when(z - d >= 0)(lambda: from_line(k, z - d, z < nz - 1, up))
        pl.when(z + d < nz)(lambda: from_line(k, z + d, z > 0, down))
        pl.when(z - d + 1 >= 0)(lambda: from_side(k, z - d + 1))
        pl.when((d > 1) & (z + d - 1 < nz))(lambda: from_side(k, z + d - 1))
        pl.when(m == 0)(lambda: stream(0).wait())
        pl.when(m == 2)(lambda: stream(1).wait())
        cut = NSN + 4
        low, high = jnp.where(m % 2 == 0, 0, cut), jnp.where(m % 2 == 0, cut, cut + 4)
        pl.when(m < 2)(lambda: entries(low, high, (0,), True))
        pl.when((m >= 2) & (m < 4))(lambda: entries(low, high, (1,), False))
        entries(done_by(m - 1), done_by(m), (0, 1), True)
        return carry

    lax.fori_loop(0, steps, step, 0)
    start_swaps(1)

    def scatter(k, d):
        to = (row + d) % n
        code = pltpu.make_async_remote_copy(
            src_ref=codes.at[k, to], dst_ref=got_codes.at[k, d],
            send_sem=r_send.at[k, d], recv_sem=r_recv.at[k, d],
            device_id={"row": to}, device_id_type=MESH)
        scale = pltpu.make_async_remote_copy(
            src_ref=scales.at[k, to], dst_ref=got_scales.at[k, d],
            send_sem=rs_send.at[k, d], recv_sem=rs_recv.at[k, d],
            device_id={"row": to}, device_id_type=MESH)
        return code, scale

    def spread(k, d, owner):
        to = (row + d) % n
        code = pltpu.make_async_remote_copy(
            src_ref=all_codes.at[k, owner], dst_ref=all_codes.at[k, owner],
            send_sem=b_send.at[k, d], recv_sem=b_recv.at[k, d],
            device_id={"row": to}, device_id_type=MESH)
        scale = pltpu.make_async_remote_copy(
            src_ref=all_scales.at[k, owner], dst_ref=all_scales.at[k, owner],
            send_sem=bs_send.at[k, d], recv_sem=bs_recv.at[k, d],
            device_id={"row": to}, device_id_type=MESH)
        return code, scale

    width = 2 * BLK
    for k in range(NSN):
        def correct(s, carry, k=k):
            swap(k, s).wait_recv()
            own[strip(k, s)] += recv[strip(k, s)]
            left, right = [], []
            for u in range(group):
                t = s * group + u
                j = local_pick[k, t]
                scale = local_keep[k, t]
                for p in range(2):
                    left.append(jnp.concatenate([g_ref[0, k, p, j], g_ref[1, k, p, j]], axis=1))
                real = own[k, 0, aligned(t * BLK, BLK), :] * scale
                imag = own[k, 1, aligned(t * BLK, BLK), :] * scale
                right.append(jnp.concatenate([real, imag], axis=1))
                right.append(jnp.concatenate([-imag, real], axis=1))
            factor = jnp.concatenate(left, axis=0)
            wide = jnp.concatenate(right, axis=0)
            total = None
            for _ in range(2):
                piece = wide.astype(jnp.bfloat16)
                wide = wide - piece.astype(jnp.float32)
                term = lax.dot_general(factor, piece, (((0,), (0,)), ((), ())),
                                       preferred_element_type=jnp.float32)
                total = term if total is None else total + term
            mine[2 * k * width:(2 * k + 1) * width, :] += total[:, :BLK]
            mine[(2 * k + 1) * width:(2 * k + 2) * width, :] += total[:, BLK:]
            return carry

        lax.fori_loop(0, strips, correct, 0)

        codes[k], scales[k] = coded(mine[k * n * size:(k + 1) * n * size, :].reshape(codes.shape[1:]))
        for d in range(1, n):
            for c in scatter(k, d):
                c.start()

    for k in range(NSN):
        own_diag(k).wait()
        total = mine[place(k, row), :]
        for d in range(1, n):
            for c in scatter(k, d):
                c.wait_recv()
            total = total + decoded(got_codes[k, d], got_scales[k, d])
        all_codes[k, row], all_scales[k, row] = coded(diag[k].astype(jnp.float32) - total)
        for d in range(1, n):
            for c in spread(k, d, row):
                c.start()

    for k in range(NSN):
        for r in range(n):
            sib(slot(col, k, r), col, k, r).wait_send()
        for zz in range(nz):
            side(here(k, zz, y), k, zz, y).wait_send()
            pl.when(((zz < z) & (z < nz - 1)) | ((zz > z) & (z > 0)))(
                lambda k=k, zz=zz: line(here(k, zz, y), k, zz, up).wait_send())
        pl.when(z < nz - 1)(lambda k=k: first_up(k).wait_send())
        pl.when(z > 0)(lambda k=k: first_down(k).wait_send())
        def drain(s, carry, k=k):
            swap(k, s).wait_send()
            return carry

        lax.fori_loop(0, strips, drain, 0)
        for d in range(1, n):
            for c in scatter(k, d) + spread(k, d, row):
                c.wait_send()

    for k in range(NSN):
        for d in range(1, n):
            for c in spread(k, d, (row - d) % n):
                c.wait_recv()

        sum_ref[k * n * size:(k + 1) * n * size, :] = decoded(all_codes[k], all_scales[k]).reshape(n * size, sum_ref.shape[1])


def local(n, inverse_pairs, factor_rows, diag_blocks, row_lists, block_order):
    rows, cols = inverse_pairs.shape[1:]
    blocks_row, blocks_col = rows // BLK, cols // BLK
    listed = row_lists.shape[1]
    order = block_order.reshape(1, -1)

    ny = 2 if n % 2 == 0 else 1
    nz = n // ny
    span, half = factor_rows.shape[2:]
    size = NSN * 2 * 2 * half
    piece = size // (NSN * n)
    per = max(1, span // BLK)
    shards = factor_rows.reshape(NSN, 2, per, BLK, half) if span >= BLK else factor_rows
    dma = pltpu.SemaphoreType.DMA
    side = (NSN, 2, rows, half)
    values, schur = pl.pallas_call(
        functools.partial(kernel, n, ny),
        out_shape=(pltpu.VMEM(side, jnp.float32), pltpu.VMEM((size, half), jnp.float32)),
        in_specs=[ANY, ANY, ANY, ANY, ANY],
        out_specs=(VMEM, VMEM),
        scratch_shapes=[
            pltpu.SMEM((NSN, listed), jnp.int32),
            pltpu.SMEM(order.shape, jnp.int32),
            pltpu.VMEM((NSN, listed), jnp.int32),
            pltpu.VMEM(order.shape, jnp.int32),
            pltpu.SMEM((NSN, listed), jnp.int32),
            pltpu.SMEM((NSN, listed), jnp.float32),
            pltpu.SMEM((NSN, blocks_row), jnp.int32),
            pltpu.SMEM((NSN, blocks_row), jnp.float32),
            pltpu.VMEM((2, rows // 2, cols), jnp.bfloat16),
            pltpu.VMEM((2, rows // 2, cols), jnp.bfloat16),
            pltpu.VMEM((2, NSN, 2, listed, BLK, half), jnp.bfloat16),
            pltpu.VMEM(side, jnp.float32),
            pltpu.VMEM(side, jnp.float32),
            pltpu.VMEM((per * 2 * BLK, 4 * BLK), jnp.bfloat16),
            pltpu.VMEM((size, half), jnp.float32),
            pltpu.VMEM((NSN, n, piece, half), jnp.int16), pltpu.VMEM((NSN, n, 1, half), jnp.float32),
            pltpu.VMEM((NSN, n, piece, half), jnp.int16), pltpu.VMEM((NSN, n, 1, half), jnp.float32),
            pltpu.VMEM((NSN, n, piece, half), jnp.int16), pltpu.VMEM((NSN, n, 1, half), jnp.float32),
            pltpu.VMEM((NSN, piece, half), jnp.bfloat16),
            dma((4,)), dma((2,)), dma((NSN,)), dma((NSN,)), dma((NSN, nz + 2)), dma((NSN, nz)),
            dma((NSN, nz)), dma((NSN, nz)), dma((NSN, n)), dma((NSN, n)),
            dma((NSN, blocks_row)), dma((NSN, blocks_row)), dma((NSN, blocks_row)),
            dma((NSN, n)), dma((NSN, n)), dma((NSN, n)), dma((NSN, n)),
            dma((NSN, n)), dma((NSN, n)), dma((NSN, n)), dma((NSN, n)),
        ],
        compiler_params=pltpu.CompilerParams(
            collective_id=0, has_side_effects=True, vmem_limit_bytes=58000000),
        name="inversion_step",
    )(row_lists, order, shards, inverse_pairs, diag_blocks.reshape(size, half))
    return (values, schur.reshape(diag_blocks.shape))


def solution(mesh):
    in_specs = (
        P("pole", "row", "col"),
        P("pole", None, "row", "col"),
        P("pole", None, None, "col"),
        P(),
        P(),
    )
    out_specs = (P("pole", None, "row", "col"), P("pole", None, None, "col"))
    return jax.shard_map(functools.partial(local, mesh.shape["row"]), mesh=mesh, in_specs=in_specs,
                         out_specs=out_specs, check_vma=False)
```

```python
import functools

import jax
import jax.numpy as jnp
from jax import lax
from jax.experimental import pallas as pl
from jax.experimental.pallas import tpu as pltpu
from jax.sharding import PartitionSpec as P

NSN = 2
BLK = 128
MESH = pl.DeviceIdType.MESH
ANY = pl.BlockSpec(memory_space=pl.ANY)
VMEM = pl.BlockSpec(memory_space=pltpu.VMEM)
SMEM = pl.BlockSpec(memory_space=pltpu.SMEM)


def aligned(start, size):
    return pl.ds(pl.multiple_of(start, size), size)


def index_tables(lists_s, order_s, lists_v, order_v, pick, keep, local_pick, local_keep, first, row, blocks_col, blocks_row):
    order = order_v[...]
    storage = lax.broadcasted_iota(jnp.int32, order.shape, 1)
    for k in range(lists_s.shape[0]):
        for j in range(lists_s.shape[1]):
            at = jnp.sum(jnp.where(order == lists_s[k, j], storage, 0)) - first
            inside = (at >= 0) & (at < blocks_col)
            pick[k, j] = jnp.clip(at, 0, blocks_col - 1)
            keep[k, j] = jnp.where(inside, 1.0, 0.0)
        listed = lists_v[k:k + 1, :]
        entry = lax.broadcasted_iota(jnp.int32, listed.shape, 1) + 1
        for t in range(blocks_row):
            found = jnp.sum(jnp.where(listed == order_s[0, row * blocks_row + t], entry, 0))
            local_pick[k, t] = jnp.clip(found - 1, 0, lists_s.shape[1] - 1)
            local_keep[k, t] = jnp.where(found > 0, 1.0, 0.0)


def coded(value):
    most = jnp.maximum(jnp.max(jnp.abs(value), axis=-2, keepdims=True), 1e-33)
    return jnp.round(value * (32767.0 / most)).astype(jnp.int32).astype(jnp.int16), most * (1.0 / 32767.0)


def decoded(code, scale):
    return code.astype(jnp.int32).astype(jnp.float32) * scale


def kernel(n, ny, lists_ref, order_ref, x_ref, a_ref, diag_ref, own, sum_ref,
           lists_s, order_s, lists_v, order_v, pick, keep, local_pick, local_keep, a_top, a_low, g_ref, oth, recv, bbuf, mine, codes, scales, got_codes, got_scales, all_codes, all_scales, diag,
           t_sem, a_sem, loc_sem, diag_sem, z_send, z_recv, y_send, y_recv, x_send, s_send, s_recv,
           v_send, v_recv, o_sem, r_send, r_recv, rs_send, rs_recv, b_send, b_recv, bs_send, bs_recv):
    nz = n // ny
    span = g_ref.shape[3] * BLK // n
    rows = a_ref.shape[1]
    blocks_col = a_ref.shape[2] // BLK
    blocks_row = rows // BLK
    tall = a_top.shape[1]
    per = max(1, span // BLK)
    unit = min(span, BLK)
    row = lax.axis_index("row")
    col = lax.axis_index("col")
    z = row // ny
    y = row % ny
    oy = ny - 1 - y
    sibling = {"col": 1 - col}
    up = {"row": row + ny}
    down = {"row": row - ny}
    across = {"row": z * ny + oy}
    size = sum_ref.shape[0] // (NSN * n)

    def place(k, r):
        return aligned(k * n * size + r * size, size)

    def stream(half):
        a_half = a_low if half else a_top
        return pltpu.make_async_copy(a_ref.at[:, half * tall:(half + 1) * tall], a_half, a_sem.at[half])

    def slot(c, k, r):
        if span >= BLK:
            return g_ref.at[c, k, :, pl.ds(r * per, per)]
        return g_ref.at[c, k, :, r * span // BLK, aligned(r * span % BLK, span)]

    def local(k):
        return pltpu.make_async_copy(x_ref.at[k], slot(col, k, row), loc_sem.at[k])

    def own_diag(k):
        return pltpu.make_async_copy(diag_ref.at[place(k, row)], diag.at[k], diag_sem.at[k])

    for k in range(NSN):
        local(k).start()
    tables = [pltpu.make_async_copy(*pair, t_sem.at[i]) for i, pair in enumerate(
        ((lists_ref, lists_s), (order_ref, order_s), (lists_ref, lists_v), (order_ref, order_v)))]
    for c in tables:
        c.start()
    for half in range(2):
        stream(half).start()

    barrier = pltpu.get_barrier_semaphore()
    pl.semaphore_signal(barrier, inc=1, device_id=sibling, device_id_type=MESH)
    pl.semaphore_signal(barrier, inc=1, device_id=across, device_id_type=MESH)
    pl.when(z < nz - 1)(lambda: pl.semaphore_signal(barrier, inc=1, device_id=up, device_id_type=MESH))
    pl.when(z > 0)(lambda: pl.semaphore_signal(barrier, inc=1, device_id=down, device_id_type=MESH))
    pl.semaphore_wait(barrier, 2 + jnp.where(z < nz - 1, 1, 0) + jnp.where(z > 0, 1, 0))

    def copy(src, c, k, r, send, got, target):
        return pltpu.make_async_remote_copy(
            src_ref=src, dst_ref=slot(c, k, r), send_sem=send, recv_sem=got,
            device_id=target, device_id_type=MESH)

    def line(src, k, zz, target):
        return copy(src, col, k, zz * ny + y, z_send.at[k, zz], z_recv.at[k, zz], target)

    def side(src, k, zz, yy):
        return copy(src, col, k, zz * ny + yy, y_send.at[k, zz], y_recv.at[k, zz], across)

    def sib(src, c, k, r):
        return copy(src, c, k, r, s_send.at[k, r], s_recv.at[k, r], sibling)

    def here(k, zz, yy):
        return slot(col, k, zz * ny + yy)

    def first_up(k):
        return copy(x_ref.at[k], col, k, row, z_send.at[k, nz], z_recv.at[k, z], up)

    def first_down(k):
        return copy(x_ref.at[k], col, k, row, z_send.at[k, nz + 1], z_recv.at[k, z], down)

    for k in range(NSN):
        side(x_ref.at[k], k, z, y).start()
        pl.when(z < nz - 1)(lambda k=k: first_up(k).start())
        pl.when(z > 0)(lambda k=k: first_down(k).start())
        sib(x_ref.at[k], col, k, row).start()
    for k in range(NSN):
        own_diag(k).start()
    for c in tables:
        c.wait()
    index_tables(lists_s, order_s, lists_v, order_v, pick, keep, local_pick, local_keep,
                 col * blocks_col, row, blocks_col, blocks_row)
    own[...] = jnp.zeros_like(own)
    oth[...] = jnp.zeros_like(oth)
    mine[...] = jnp.zeros_like(mine)
    for k in range(NSN):
        local(k).wait()

    def from_line(k, zz, forward, target):
        line(here(k, zz, y), k, zz, target).wait_recv()

        @pl.when(forward)
        def _():
            line(here(k, zz, y), k, zz, target).start()

        pl.when(crosses(k, zz))(lambda: side(here(k, zz, y), k, zz, y).start())
        sib(here(k, zz, y), col, k, zz * ny + y).start()

    def crosses(k, zz):
        return (k < NSN - 1) | ((zz > 0) & (zz < nz - 1))

    def relay(end):
        zz = end * (nz - 1)
        return copy(here(NSN - 1, zz, oy), col, NSN - 1, zz * ny + oy, x_send.at[end], y_recv.at[NSN - 1, zz],
                    down if end else up)

    def arrived(k, zz):
        side(here(k, zz, oy), k, zz, oy).wait_recv()
        pl.when((k == NSN - 1) & (zz == 0) & (z < nz - 1))(lambda: relay(0).start())
        pl.when((k == NSN - 1) & (zz == nz - 1) & (z > 0))(lambda: relay(1).start())
        sib(here(k, zz, oy), col, k, zz * ny + oy).start()

    def from_side(k, zz):
        pl.when((zz == z) | crosses(k, zz))(lambda: arrived(k, zz))

    def from_relay(m):
        for zz in (0, nz - 1):
            away = jnp.abs(z - zz)
            due = jnp.where(away < 3, away + 2, 2 * away + 1)
            pl.when((away > 0) & (m == due))(lambda zz=zz: arrived(NSN - 1, zz))

    outs = (own, oth)

    def multiply(k, r, halves, fresh):
        if fresh:
            sib(slot(1 - col, k, r), 1 - col, k, r).wait_recv()
        if unit < BLK:
            bbuf[...] = jnp.zeros_like(bbuf)
        for e in range(per):
            start = r * span + e * BLK
            scale = keep[k, start // BLK]
            base = e * 2 * BLK
            if unit < BLK:
                shift = start % BLK
                top = aligned(base + shift, unit)
                low = aligned(base + BLK + shift, unit)
            else:
                top = pl.ds(base, unit)
                low = pl.ds(base + BLK, unit)
            for rel in range(2):
                c = col if rel == 0 else 1 - col
                at = pl.ds(0, unit) if unit == BLK else aligned(start % BLK, unit)
                real = (g_ref[c, k, 0, start // BLK, at, :].astype(jnp.float32) * scale).astype(jnp.bfloat16)
                imag = (g_ref[c, k, 1, start // BLK, at, :].astype(jnp.float32) * scale).astype(jnp.bfloat16)
                left = rel * 2 * BLK
                bbuf[top, left:left + BLK] = -real
                bbuf[top, left + BLK:left + 2 * BLK] = -imag
                bbuf[low, left:left + BLK] = imag
                bbuf[low, left + BLK:left + 2 * BLK] = -real

        at = slice(halves[0] * tall, (halves[-1] + 1) * tall)
        left = []
        for half in halves:
            a_half = a_low if half else a_top
            pieces = []
            for e in range(per):
                block = pl.ds(pick[k, (r * span + e * BLK) // BLK] * BLK, BLK)
                pieces += [a_half[0, :, block], a_half[1, :, block]]
            left.append(jnp.concatenate(pieces, axis=1))
        left = jnp.concatenate(left, axis=0) if len(left) > 1 else left[0]
        for rel in range(2):
            found = jnp.dot(left, bbuf[:, rel * 2 * BLK:(rel + 1) * 2 * BLK],
                            preferred_element_type=jnp.float32)
            outs[rel][k, 0, at, :] += found[:, :BLK]
            outs[rel][k, 1, at, :] += found[:, BLK:]

    group = 3 if blocks_row % 3 == 0 else 1
    strips = blocks_row // group
    high = group * BLK

    def strip(k, s):
        return k, slice(None), aligned(s * high, high)

    def swap(k, s):
        return pltpu.make_async_remote_copy(
            src_ref=oth.at[strip(k, s)], dst_ref=recv.at[strip(k, s)], send_sem=v_send.at[k, s], recv_sem=v_recv.at[k, s],
            device_id=sibling, device_id_type=MESH)

    def start_swaps(k):
        def one(s, carry):
            swap(k, s).start()
            return carry
        lax.fori_loop(0, strips, one, 0)


    steps = max(2 * nz, 4)

    def entries(low, high, halves, fresh):
        def entry(e, carry):
            g = (e - NSN) // 4
            q = (e - NSN) % 4
            away = g // 2 + 1 - q // 2
            mine_first = e < NSN
            k = jnp.where(mine_first, e, g % 2)
            zz = z + jnp.where(mine_first, 0, jnp.where(q % 2 == 0, -away, away))
            yy = jnp.where(mine_first | (q // 2 == 0), y, oy)
            valid = mine_first | ((zz >= 0) & (zz < nz) & ((away > 0) | (q % 2 == 0)))
            pl.when(valid)(lambda: multiply(k, zz * ny + yy, halves, fresh))
            return carry

        lax.fori_loop(low, high, entry, 0)

    def done_by(m):
        ahead = NSN + 4 * jnp.where(m >= steps - 2, m + 1, m)
        return jnp.where(m < 3, NSN + 8, ahead)

    def step(m, carry):
        d = m // 2 + 1
        k = m % 2
        from_relay(m)
        pl.when(z - d >= 0)(lambda: from_line(k, z - d, z < nz - 1, up))
        pl.when(z + d < nz)(lambda: from_line(k, z + d, z > 0, down))
        pl.when(z - d + 1 >= 0)(lambda: from_side(k, z - d + 1))
        pl.when((d > 1) & (z + d - 1 < nz))(lambda: from_side(k, z + d - 1))
        pl.when(m == 0)(lambda: stream(0).wait())
        pl.when(m == 2)(lambda: stream(1).wait())
        cut = NSN + 4
        low, high = jnp.where(m % 2 == 0, 0, cut), jnp.where(m % 2 == 0, cut, cut + 4)
        pl.when(m < 2)(lambda: entries(low, high, (0,), True))
        pl.when((m >= 2) & (m < 4))(lambda: entries(low, high, (1,), False))
        pl.when(m == steps - 1)(lambda: start_swaps(0))
        entries(done_by(m - 1), done_by(m), (0, 1), True)
        return carry

    lax.fori_loop(0, steps, step, 0)
    start_swaps(1)

    def scatter(k, d):
        to = (row + d) % n
        code = pltpu.make_async_remote_copy(
            src_ref=codes.at[k, to], dst_ref=got_codes.at[k, d],
            send_sem=r_send.at[k, d], recv_sem=r_recv.at[k, d],
            device_id={"row": to}, device_id_type=MESH)
        scale = pltpu.make_async_remote_copy(
            src_ref=scales.at[k, to], dst_ref=got_scales.at[k, d],
            send_sem=rs_send.at[k, d], recv_sem=rs_recv.at[k, d],
            device_id={"row": to}, device_id_type=MESH)
        return code, scale

    def spread(k, d, owner):
        to = (row + d) % n
        code = pltpu.make_async_remote_copy(
            src_ref=all_codes.at[k, owner], dst_ref=all_codes.at[k, owner],
            send_sem=b_send.at[k, d], recv_sem=b_recv.at[k, d],
            device_id={"row": to}, device_id_type=MESH)
        scale = pltpu.make_async_remote_copy(
            src_ref=all_scales.at[k, owner], dst_ref=all_scales.at[k, owner],
            send_sem=bs_send.at[k, d], recv_sem=bs_recv.at[k, d],
            device_id={"row": to}, device_id_type=MESH)
        return code, scale

    width = 2 * BLK
    for k in range(NSN):
        def correct(s, carry, k=k):
            swap(k, s).wait_recv()
            own[strip(k, s)] += recv[strip(k, s)]
            left, right = [], []
            for u in range(group):
                t = s * group + u
                j = local_pick[k, t]
                scale = local_keep[k, t]
                for p in range(2):
                    left.append(jnp.concatenate([g_ref[0, k, p, j], g_ref[1, k, p, j]], axis=1))
                real = own[k, 0, aligned(t * BLK, BLK), :] * scale
                imag = own[k, 1, aligned(t * BLK, BLK), :] * scale
                right.append(jnp.concatenate([real, imag], axis=1))
                right.append(jnp.concatenate([-imag, real], axis=1))
            factor = jnp.concatenate(left, axis=0)
            wide = jnp.concatenate(right, axis=0)
            total = None
            for _ in range(2):
                piece = wide.astype(jnp.bfloat16)
                wide = wide - piece.astype(jnp.float32)
                term = lax.dot_general(factor, piece, (((0,), (0,)), ((), ())),
                                       preferred_element_type=jnp.float32)
                total = term if total is None else total + term
            mine[2 * k * width:(2 * k + 1) * width, :] += total[:, :BLK]
            mine[(2 * k + 1) * width:(2 * k + 2) * width, :] += total[:, BLK:]
            return carry

        lax.fori_loop(0, strips, correct, 0)

        codes[k], scales[k] = coded(mine[k * n * size:(k + 1) * n * size, :].reshape(codes.shape[1:]))
        for d in range(1, n):
            for c in scatter(k, d):
                c.start()

    for k in range(NSN):
        own_diag(k).wait()
        total = mine[place(k, row), :]
        for d in range(1, n):
            for c in scatter(k, d):
                c.wait_recv()
            total = total + decoded(got_codes[k, d], got_scales[k, d])
        all_codes[k, row], all_scales[k, row] = coded(diag[k].astype(jnp.float32) - total)
        for d in range(1, n):
            for c in spread(k, d, row):
                c.start()

    pl.when(z < nz - 1)(lambda: relay(0).wait_send())
    pl.when(z > 0)(lambda: relay(1).wait_send())
    for k in range(NSN):
        for r in range(n):
            sib(slot(col, k, r), col, k, r).wait_send()
        for zz in range(nz):
            pl.when((z == zz) | crosses(k, zz))(lambda k=k, zz=zz: side(here(k, zz, y), k, zz, y).wait_send())
            pl.when(((zz < z) & (z < nz - 1)) | ((zz > z) & (z > 0)))(
                lambda k=k, zz=zz: line(here(k, zz, y), k, zz, up).wait_send())
        pl.when(z < nz - 1)(lambda k=k: first_up(k).wait_send())
        pl.when(z > 0)(lambda k=k: first_down(k).wait_send())
        def drain(s, carry, k=k):
            swap(k, s).wait_send()
            return carry

        lax.fori_loop(0, strips, drain, 0)
        for d in range(1, n):
            for c in scatter(k, d) + spread(k, d, row):
                c.wait_send()

    for k in range(NSN):
        for d in range(1, n):
            for c in spread(k, d, (row - d) % n):
                c.wait_recv()

        sum_ref[k * n * size:(k + 1) * n * size, :] = decoded(all_codes[k], all_scales[k]).reshape(n * size, sum_ref.shape[1])


def local(n, inverse_pairs, factor_rows, diag_blocks, row_lists, block_order):
    rows, cols = inverse_pairs.shape[1:]
    blocks_row, blocks_col = rows // BLK, cols // BLK
    listed = row_lists.shape[1]
    order = block_order.reshape(1, -1)

    ny = 2 if n % 2 == 0 else 1
    nz = n // ny
    span, half = factor_rows.shape[2:]
    size = NSN * 2 * 2 * half
    piece = size // (NSN * n)
    per = max(1, span // BLK)
    shards = factor_rows.reshape(NSN, 2, per, BLK, half) if span >= BLK else factor_rows
    dma = pltpu.SemaphoreType.DMA
    side = (NSN, 2, rows, half)
    values, schur = pl.pallas_call(
        functools.partial(kernel, n, ny),
        out_shape=(pltpu.VMEM(side, jnp.float32), pltpu.VMEM((size, half), jnp.float32)),
        in_specs=[ANY, ANY, ANY, ANY, ANY],
        out_specs=(VMEM, VMEM),
        scratch_shapes=[
            pltpu.SMEM((NSN, listed), jnp.int32),
            pltpu.SMEM(order.shape, jnp.int32),
            pltpu.VMEM((NSN, listed), jnp.int32),
            pltpu.VMEM(order.shape, jnp.int32),
            pltpu.SMEM((NSN, listed), jnp.int32),
            pltpu.SMEM((NSN, listed), jnp.float32),
            pltpu.SMEM((NSN, blocks_row), jnp.int32),
            pltpu.SMEM((NSN, blocks_row), jnp.float32),
            pltpu.VMEM((2, rows // 2, cols), jnp.bfloat16),
            pltpu.VMEM((2, rows // 2, cols), jnp.bfloat16),
            pltpu.VMEM((2, NSN, 2, listed, BLK, half), jnp.bfloat16),
            pltpu.VMEM(side, jnp.float32),
            pltpu.VMEM(side, jnp.float32),
            pltpu.VMEM((per * 2 * BLK, 4 * BLK), jnp.bfloat16),
            pltpu.VMEM((size, half), jnp.float32),
            pltpu.VMEM((NSN, n, piece, half), jnp.int16), pltpu.VMEM((NSN, n, 1, half), jnp.float32),
            pltpu.VMEM((NSN, n, piece, half), jnp.int16), pltpu.VMEM((NSN, n, 1, half), jnp.float32),
            pltpu.VMEM((NSN, n, piece, half), jnp.int16), pltpu.VMEM((NSN, n, 1, half), jnp.float32),
            pltpu.VMEM((NSN, piece, half), jnp.bfloat16),
            dma((4,)), dma((2,)), dma((NSN,)), dma((NSN,)), dma((NSN, nz + 2)), dma((NSN, nz)),
            dma((NSN, nz)), dma((NSN, nz)), dma((2,)), dma((NSN, n)), dma((NSN, n)),
            dma((NSN, blocks_row)), dma((NSN, blocks_row)), dma((NSN, blocks_row)),
            dma((NSN, n)), dma((NSN, n)), dma((NSN, n)), dma((NSN, n)),
            dma((NSN, n)), dma((NSN, n)), dma((NSN, n)), dma((NSN, n)),
        ],
        compiler_params=pltpu.CompilerParams(
            collective_id=0, has_side_effects=True, vmem_limit_bytes=58000000),
        name="inversion_step",
    )(row_lists, order, shards, inverse_pairs, diag_blocks.reshape(size, half))
    return (values, schur.reshape(diag_blocks.shape))


def solution(mesh):
    in_specs = (
        P("pole", "row", "col"),
        P("pole", None, "row", "col"),
        P("pole", None, None, "col"),
        P(),
        P(),
    )
    out_specs = (P("pole", None, "row", "col"), P("pole", None, None, "col"))
    return jax.shard_map(functools.partial(local, mesh.shape["row"]), mesh=mesh, in_specs=in_specs,
                         out_specs=out_specs, check_vma=False)
```

```python
import functools

import jax
import jax.numpy as jnp
from jax import lax
from jax.experimental import pallas as pl
from jax.experimental.pallas import tpu as pltpu
from jax.sharding import PartitionSpec as P

NSN = 2
BLK = 128
MESH = pl.DeviceIdType.MESH
ANY = pl.BlockSpec(memory_space=pl.ANY)
VMEM = pl.BlockSpec(memory_space=pltpu.VMEM)
SMEM = pl.BlockSpec(memory_space=pltpu.SMEM)


def aligned(start, size):
    return pl.ds(pl.multiple_of(start, size), size)


def index_tables(lists_s, order_s, lists_v, order_v, pick, keep, local_pick, local_keep, first, row, blocks_col, blocks_row):
    order = order_v[...]
    storage = lax.broadcasted_iota(jnp.int32, order.shape, 1)
    for k in range(lists_s.shape[0]):
        for j in range(lists_s.shape[1]):
            at = jnp.sum(jnp.where(order == lists_s[k, j], storage, 0)) - first
            inside = (at >= 0) & (at < blocks_col)
            pick[k, j] = jnp.clip(at, 0, blocks_col - 1)
            keep[k, j] = jnp.where(inside, 1.0, 0.0)
        listed = lists_v[k:k + 1, :]
        entry = lax.broadcasted_iota(jnp.int32, listed.shape, 1) + 1
        for t in range(blocks_row):
            found = jnp.sum(jnp.where(listed == order_s[0, row * blocks_row + t], entry, 0))
            local_pick[k, t] = jnp.clip(found - 1, 0, lists_s.shape[1] - 1)
            local_keep[k, t] = jnp.where(found > 0, 1.0, 0.0)


def coded(value):
    most = jnp.maximum(jnp.max(jnp.abs(value), axis=-2, keepdims=True), 1e-33)
    return jnp.round(value * (32767.0 / most)).astype(jnp.int32).astype(jnp.int16), most * (1.0 / 32767.0)


def decoded(code, scale):
    return code.astype(jnp.int32).astype(jnp.float32) * scale


def kernel(n, ny, lists_ref, order_ref, x_ref, a_ref, diag_ref, own, sum_ref,
           lists_s, order_s, lists_v, order_v, pick, keep, local_pick, local_keep, a_top, a_low, g_ref, oth, recv, bbuf, mine, codes, scales, got_codes, got_scales, all_codes, all_scales, diag,
           t_sem, a_sem, loc_sem, diag_sem, z_send, z_recv, y_send, y_recv, x_send, s_send, s_recv,
           v_send, v_recv, o_sem, r_send, r_recv, rs_send, rs_recv, b_send, b_recv, bs_send, bs_recv):
    nz = n // ny
    span = g_ref.shape[3] * BLK // n
    rows = a_ref.shape[1]
    blocks_col = a_ref.shape[2] // BLK
    blocks_row = rows // BLK
    tall = a_top.shape[1]
    per = max(1, span // BLK)
    unit = min(span, BLK)
    row = lax.axis_index("row")
    col = lax.axis_index("col")
    z = row // ny
    y = row % ny
    oy = ny - 1 - y
    sibling = {"col": 1 - col}
    up = {"row": row + ny}
    down = {"row": row - ny}
    across = {"row": z * ny + oy}
    size = sum_ref.shape[0] // (NSN * n)

    def place(k, r):
        return aligned(k * n * size + r * size, size)

    def stream(half):
        a_half = a_low if half else a_top
        return pltpu.make_async_copy(a_ref.at[:, half * tall:(half + 1) * tall], a_half, a_sem.at[half])

    def slot(c, k, r):
        if span >= BLK:
            return g_ref.at[c, k, :, pl.ds(r * per, per)]
        return g_ref.at[c, k, :, r * span // BLK, aligned(r * span % BLK, span)]

    def local(k):
        return pltpu.make_async_copy(x_ref.at[k], slot(col, k, row), loc_sem.at[k])

    def own_diag(k):
        return pltpu.make_async_copy(diag_ref.at[place(k, row)], diag.at[k], diag_sem.at[k])

    for k in range(NSN):
        local(k).start()
    tables = [pltpu.make_async_copy(*pair, t_sem.at[i]) for i, pair in enumerate(
        ((lists_ref, lists_s), (order_ref, order_s), (lists_ref, lists_v), (order_ref, order_v)))]
    for c in tables:
        c.start()
    for half in range(2):
        stream(half).start()

    barrier = pltpu.get_barrier_semaphore()
    pl.semaphore_signal(barrier, inc=1, device_id=sibling, device_id_type=MESH)
    pl.semaphore_signal(barrier, inc=1, device_id=across, device_id_type=MESH)
    pl.when(z < nz - 1)(lambda: pl.semaphore_signal(barrier, inc=1, device_id=up, device_id_type=MESH))
    pl.when(z > 0)(lambda: pl.semaphore_signal(barrier, inc=1, device_id=down, device_id_type=MESH))
    pl.semaphore_wait(barrier, 2 + jnp.where(z < nz - 1, 1, 0) + jnp.where(z > 0, 1, 0))

    def copy(src, c, k, r, send, got, target):
        return pltpu.make_async_remote_copy(
            src_ref=src, dst_ref=slot(c, k, r), send_sem=send, recv_sem=got,
            device_id=target, device_id_type=MESH)

    def line(src, k, zz, target):
        return copy(src, col, k, zz * ny + y, z_send.at[k, zz], z_recv.at[k, zz], target)

    def side(src, k, zz, yy):
        return copy(src, col, k, zz * ny + yy, y_send.at[k, zz], y_recv.at[k, zz], across)

    def sib(src, c, k, r):
        return copy(src, c, k, r, s_send.at[k, r], s_recv.at[k, r], sibling)

    def here(k, zz, yy):
        return slot(col, k, zz * ny + yy)

    def first_up(k):
        return copy(x_ref.at[k], col, k, row, z_send.at[k, nz], z_recv.at[k, z], up)

    def first_down(k):
        return copy(x_ref.at[k], col, k, row, z_send.at[k, nz + 1], z_recv.at[k, z], down)

    for k in range(NSN):
        side(x_ref.at[k], k, z, y).start()
        pl.when(z < nz - 1)(lambda k=k: first_up(k).start())
        pl.when(z > 0)(lambda k=k: first_down(k).start())
        sib(x_ref.at[k], col, k, row).start()
    for k in range(NSN):
        own_diag(k).start()
    for c in tables:
        c.wait()
    index_tables(lists_s, order_s, lists_v, order_v, pick, keep, local_pick, local_keep,
                 col * blocks_col, row, blocks_col, blocks_row)
    own[...] = jnp.zeros_like(own)
    oth[...] = jnp.zeros_like(oth)
    mine[...] = jnp.zeros_like(mine)
    for k in range(NSN):
        local(k).wait()

    def from_line(k, zz, forward, target):
        line(here(k, zz, y), k, zz, target).wait_recv()

        @pl.when(forward)
        def _():
            line(here(k, zz, y), k, zz, target).start()

        pl.when(crosses(k, zz))(lambda: side(here(k, zz, y), k, zz, y).start())
        sib(here(k, zz, y), col, k, zz * ny + y).start()

    def crosses(k, zz):
        return (k < NSN - 1) | ((zz > 0) & (zz < nz - 1))

    def relay(end):
        zz = end * (nz - 1)
        return copy(here(NSN - 1, zz, oy), col, NSN - 1, zz * ny + oy, x_send.at[end], y_recv.at[NSN - 1, zz],
                    down if end else up)

    def arrived(k, zz):
        side(here(k, zz, oy), k, zz, oy).wait_recv()
        pl.when((k == NSN - 1) & (zz == 0) & (z < nz - 1))(lambda: relay(0).start())
        pl.when((k == NSN - 1) & (zz == nz - 1) & (z > 0))(lambda: relay(1).start())
        sib(here(k, zz, oy), col, k, zz * ny + oy).start()

    def from_side(k, zz):
        pl.when((zz == z) | crosses(k, zz))(lambda: arrived(k, zz))

    def from_relay(m):
        for zz in (0, nz - 1):
            away = jnp.abs(z - zz)
            due = jnp.where(away < 3, away + 2, 2 * away + 1)
            pl.when((away > 0) & (m == due))(lambda zz=zz: arrived(NSN - 1, zz))

    outs = (own, oth)

    def multiply(k, r, halves, fresh):
        if fresh:
            sib(slot(1 - col, k, r), 1 - col, k, r).wait_recv()
        if unit < BLK:
            bbuf[...] = jnp.zeros_like(bbuf)
        for e in range(per):
            start = r * span + e * BLK
            scale = keep[k, start // BLK]
            base = e * 2 * BLK
            if unit < BLK:
                shift = start % BLK
                top = aligned(base + shift, unit)
                low = aligned(base + BLK + shift, unit)
            else:
                top = pl.ds(base, unit)
                low = pl.ds(base + BLK, unit)
            for rel in range(2):
                c = col if rel == 0 else 1 - col
                at = pl.ds(0, unit) if unit == BLK else aligned(start % BLK, unit)
                real = (g_ref[c, k, 0, start // BLK, at, :].astype(jnp.float32) * scale).astype(jnp.bfloat16)
                imag = (g_ref[c, k, 1, start // BLK, at, :].astype(jnp.float32) * scale).astype(jnp.bfloat16)
                left = rel * 2 * BLK
                bbuf[top, left:left + BLK] = -real
                bbuf[top, left + BLK:left + 2 * BLK] = -imag
                bbuf[low, left:left + BLK] = imag
                bbuf[low, left + BLK:left + 2 * BLK] = -real

        at = slice(halves[0] * tall, (halves[-1] + 1) * tall)
        left = []
        for half in halves:
            a_half = a_low if half else a_top
            pieces = []
            for e in range(per):
                block = pl.ds(pick[k, (r * span + e * BLK) // BLK] * BLK, BLK)
                pieces += [a_half[0, :, block], a_half[1, :, block]]
            left.append(jnp.concatenate(pieces, axis=1))
        left = jnp.concatenate(left, axis=0) if len(left) > 1 else left[0]
        for rel in range(2):
            found = jnp.dot(left, bbuf[:, rel * 2 * BLK:(rel + 1) * 2 * BLK],
                            preferred_element_type=jnp.float32)
            outs[rel][k, 0, at, :] += found[:, :BLK]
            outs[rel][k, 1, at, :] += found[:, BLK:]

    group = 2 if blocks_row % 2 == 0 else 3 if blocks_row % 3 == 0 else 1
    strips = blocks_row // group
    high = group * BLK

    def strip(k, s):
        return k, slice(None), aligned(s * high, high)

    def swap(k, s):
        return pltpu.make_async_remote_copy(
            src_ref=oth.at[strip(k, s)], dst_ref=recv.at[strip(k, s)], send_sem=v_send.at[k, s], recv_sem=v_recv.at[k, s],
            device_id=sibling, device_id_type=MESH)

    def start_swaps(k):
        def one(s, carry):
            swap(k, s).start()
            return carry
        lax.fori_loop(0, strips, one, 0)


    steps = max(2 * nz, 4)

    def entries(low, high, halves, fresh):
        def entry(e, carry):
            g = (e - NSN) // 4
            q = (e - NSN) % 4
            away = g // 2 + 1 - q // 2
            mine_first = e < NSN
            k = jnp.where(mine_first, e, g % 2)
            zz = z + jnp.where(mine_first, 0, jnp.where(q % 2 == 0, -away, away))
            yy = jnp.where(mine_first | (q // 2 == 0), y, oy)
            valid = mine_first | ((zz >= 0) & (zz < nz) & ((away > 0) | (q % 2 == 0)))
            pl.when(valid)(lambda: multiply(k, zz * ny + yy, halves, fresh))
            return carry

        lax.fori_loop(low, high, entry, 0)

    def done_by(m):
        ahead = NSN + 4 * jnp.where(m >= steps - 2, m + 1, m)
        return jnp.where(m < 3, NSN + 8, ahead)

    def step(m, carry):
        d = m // 2 + 1
        k = m % 2
        from_relay(m)
        pl.when(z - d >= 0)(lambda: from_line(k, z - d, z < nz - 1, up))
        pl.when(z + d < nz)(lambda: from_line(k, z + d, z > 0, down))
        pl.when(z - d + 1 >= 0)(lambda: from_side(k, z - d + 1))
        pl.when((d > 1) & (z + d - 1 < nz))(lambda: from_side(k, z + d - 1))
        pl.when(m == 0)(lambda: stream(0).wait())
        pl.when(m == 2)(lambda: stream(1).wait())
        cut = NSN + 4
        low, high = jnp.where(m % 2 == 0, 0, cut), jnp.where(m % 2 == 0, cut, cut + 4)
        pl.when(m < 2)(lambda: entries(low, high, (0,), True))
        pl.when((m >= 2) & (m < 4))(lambda: entries(low, high, (1,), False))
        pl.when(m == steps - 1)(lambda: start_swaps(0))
        entries(done_by(m - 1), done_by(m), (0, 1), True)
        return carry

    lax.fori_loop(0, steps, step, 0)
    start_swaps(1)

    def scatter(k, d):
        to = (row + d) % n
        code = pltpu.make_async_remote_copy(
            src_ref=codes.at[k, to], dst_ref=got_codes.at[k, d],
            send_sem=r_send.at[k, d], recv_sem=r_recv.at[k, d],
            device_id={"row": to}, device_id_type=MESH)
        scale = pltpu.make_async_remote_copy(
            src_ref=scales.at[k, to], dst_ref=got_scales.at[k, d],
            send_sem=rs_send.at[k, d], recv_sem=rs_recv.at[k, d],
            device_id={"row": to}, device_id_type=MESH)
        return code, scale

    def spread(k, d, owner):
        to = (row + d) % n
        code = pltpu.make_async_remote_copy(
            src_ref=all_codes.at[k, owner], dst_ref=all_codes.at[k, owner],
            send_sem=b_send.at[k, d], recv_sem=b_recv.at[k, d],
            device_id={"row": to}, device_id_type=MESH)
        scale = pltpu.make_async_remote_copy(
            src_ref=all_scales.at[k, owner], dst_ref=all_scales.at[k, owner],
            send_sem=bs_send.at[k, d], recv_sem=bs_recv.at[k, d],
            device_id={"row": to}, device_id_type=MESH)
        return code, scale

    width = 2 * BLK
    for k in range(NSN):
        def correct(s, carry, k=k):
            swap(k, s).wait_recv()
            own[strip(k, s)] += recv[strip(k, s)]
            left, right = [], []
            for u in range(group):
                t = s * group + u
                j = local_pick[k, t]
                scale = local_keep[k, t]
                for p in range(2):
                    left.append(jnp.concatenate([g_ref[0, k, p, j], g_ref[1, k, p, j]], axis=1))
                real = own[k, 0, aligned(t * BLK, BLK), :] * scale
                imag = own[k, 1, aligned(t * BLK, BLK), :] * scale
                right.append(jnp.concatenate([real, imag], axis=1))
                right.append(jnp.concatenate([-imag, real], axis=1))
            factor = jnp.concatenate(left, axis=0)
            wide = jnp.concatenate(right, axis=0)
            high_part = wide.astype(jnp.bfloat16)
            low_part = (wide - high_part.astype(jnp.float32)).astype(jnp.bfloat16)
            both = lax.dot_general(factor, jnp.concatenate([high_part, low_part], axis=1), (((0,), (0,)), ((), ())),
                                   preferred_element_type=jnp.float32)
            total = both[:, :width] + both[:, width:]
            mine[2 * k * width:(2 * k + 1) * width, :] += total[:, :BLK]
            mine[(2 * k + 1) * width:(2 * k + 2) * width, :] += total[:, BLK:]
            return carry

        lax.fori_loop(0, strips, correct, 0)

        codes[k], scales[k] = coded(mine[k * n * size:(k + 1) * n * size, :].reshape(codes.shape[1:]))
        for d in range(1, n):
            for c in scatter(k, d):
                c.start()

    for k in range(NSN):
        own_diag(k).wait()
        total = mine[place(k, row), :]
        for d in range(1, n):
            for c in scatter(k, d):
                c.wait_recv()
            total = total + decoded(got_codes[k, d], got_scales[k, d])
        all_codes[k, row], all_scales[k, row] = coded(diag[k].astype(jnp.float32) - total)
        for d in range(1, n):
            for c in spread(k, d, row):
                c.start()

    pl.when(z < nz - 1)(lambda: relay(0).wait_send())
    pl.when(z > 0)(lambda: relay(1).wait_send())
    for k in range(NSN):
        for r in range(n):
            sib(slot(col, k, r), col, k, r).wait_send()
        for zz in range(nz):
            pl.when((z == zz) | crosses(k, zz))(lambda k=k, zz=zz: side(here(k, zz, y), k, zz, y).wait_send())
            pl.when(((zz < z) & (z < nz - 1)) | ((zz > z) & (z > 0)))(
                lambda k=k, zz=zz: line(here(k, zz, y), k, zz, up).wait_send())
        pl.when(z < nz - 1)(lambda k=k: first_up(k).wait_send())
        pl.when(z > 0)(lambda k=k: first_down(k).wait_send())
        def drain(s, carry, k=k):
            swap(k, s).wait_send()
            return carry

        lax.fori_loop(0, strips, drain, 0)
        for d in range(1, n):
            for c in scatter(k, d) + spread(k, d, row):
                c.wait_send()

    for k in range(NSN):
        for d in range(1, n):
            for c in spread(k, d, (row - d) % n):
                c.wait_recv()

        sum_ref[k * n * size:(k + 1) * n * size, :] = decoded(all_codes[k], all_scales[k]).reshape(n * size, sum_ref.shape[1])


def local(n, inverse_pairs, factor_rows, diag_blocks, row_lists, block_order):
    rows, cols = inverse_pairs.shape[1:]
    blocks_row, blocks_col = rows // BLK, cols // BLK
    listed = row_lists.shape[1]
    order = block_order.reshape(1, -1)

    ny = 2 if n % 2 == 0 else 1
    nz = n // ny
    span, half = factor_rows.shape[2:]
    size = NSN * 2 * 2 * half
    piece = size // (NSN * n)
    per = max(1, span // BLK)
    shards = factor_rows.reshape(NSN, 2, per, BLK, half) if span >= BLK else factor_rows
    dma = pltpu.SemaphoreType.DMA
    side = (NSN, 2, rows, half)
    values, schur = pl.pallas_call(
        functools.partial(kernel, n, ny),
        out_shape=(pltpu.VMEM(side, jnp.float32), pltpu.VMEM((size, half), jnp.float32)),
        in_specs=[ANY, ANY, ANY, ANY, ANY],
        out_specs=(VMEM, VMEM),
        scratch_shapes=[
            pltpu.SMEM((NSN, listed), jnp.int32),
            pltpu.SMEM(order.shape, jnp.int32),
            pltpu.VMEM((NSN, listed), jnp.int32),
            pltpu.VMEM(order.shape, jnp.int32),
            pltpu.SMEM((NSN, listed), jnp.int32),
            pltpu.SMEM((NSN, listed), jnp.float32),
            pltpu.SMEM((NSN, blocks_row), jnp.int32),
            pltpu.SMEM((NSN, blocks_row), jnp.float32),
            pltpu.VMEM((2, rows // 2, cols), jnp.bfloat16),
            pltpu.VMEM((2, rows // 2, cols), jnp.bfloat16),
            pltpu.VMEM((2, NSN, 2, listed, BLK, half), jnp.bfloat16),
            pltpu.VMEM(side, jnp.float32),
            pltpu.VMEM(side, jnp.float32),
            pltpu.VMEM((per * 2 * BLK, 4 * BLK), jnp.bfloat16),
            pltpu.VMEM((size, half), jnp.float32),
            pltpu.VMEM((NSN, n, piece, half), jnp.int16), pltpu.VMEM((NSN, n, 1, half), jnp.float32),
            pltpu.VMEM((NSN, n, piece, half), jnp.int16), pltpu.VMEM((NSN, n, 1, half), jnp.float32),
            pltpu.VMEM((NSN, n, piece, half), jnp.int16), pltpu.VMEM((NSN, n, 1, half), jnp.float32),
            pltpu.VMEM((NSN, piece, half), jnp.bfloat16),
            dma((4,)), dma((2,)), dma((NSN,)), dma((NSN,)), dma((NSN, nz + 2)), dma((NSN, nz)),
            dma((NSN, nz)), dma((NSN, nz)), dma((2,)), dma((NSN, n)), dma((NSN, n)),
            dma((NSN, blocks_row)), dma((NSN, blocks_row)), dma((NSN, blocks_row)),
            dma((NSN, n)), dma((NSN, n)), dma((NSN, n)), dma((NSN, n)),
            dma((NSN, n)), dma((NSN, n)), dma((NSN, n)), dma((NSN, n)),
        ],
        compiler_params=pltpu.CompilerParams(
            collective_id=0, has_side_effects=True, vmem_limit_bytes=58000000),
        name="inversion_step",
    )(row_lists, order, shards, inverse_pairs, diag_blocks.reshape(size, half))
    return (values, schur.reshape(diag_blocks.shape))


def solution(mesh):
    in_specs = (
        P("pole", "row", "col"),
        P("pole", None, "row", "col"),
        P("pole", None, None, "col"),
        P(),
        P(),
    )
    out_specs = (P("pole", None, "row", "col"), P("pole", None, None, "col"))
    return jax.shard_map(functools.partial(local, mesh.shape["row"]), mesh=mesh, in_specs=in_specs,
                         out_specs=out_specs, check_vma=False)
```
